32 devices in a mesh: space: 8 (over z, x), tm: 4 (over y, core).
Axes of the slice: x: 2, y: 2, z: 4, core: 2. Of those that a mesh axis runs over, the one named last changes fastest.
Arguments:
- adjoint: bfloat16 [8, 64, 320, 512], P('tm', 'space'), may hold values from -6 to 6
- jacobian_diag: bfloat16 [8, 64, 320, 320], P('tm', 'space'), may hold values from -0.3125 to 0.3125
- jacobian_off: bfloat16 [8, 64, 2, 320, 320], P('tm', 'space'), may hold values from -0.3125 to 0.3125
- off_columns: int32 [64, 2], P('space'), may hold values from 0 to 15
- left_faces: int32 [8, 4], P('space'), may hold values from 0 to 7
- right_faces: int32 [8, 4], P('space'), may hold values from 0 to 7
- objective_grad: bfloat16 [8, 64, 320, 512], P('tm', 'space'), may hold values from -6 to 6
- pseudo_step: float32 [8, 64, 320], P('tm', 'space'), may hold values from 0.05 to 0.3
Outputs:
- adjoint_next: bfloat16 [8, 64, 320, 512], P('tm', 'space')
The draws below stay inside these ranges and needn't reach their ends.
Inputs may be any that keep to these rules, and one draw needn't show every extreme that they name: `off_columns`: codes of column blocks: below 8 a block of the same partition, then 4 slots of the previous partition's right interface, then 4 slots of the next partition's left interface. `left_faces`: block numbers within the partition, repeats possible. `right_faces`: block numbers within the partition, repeats possible.
All inputs are finite; a program needn't handle non-finite values.
Results may differ from the reference program's by a relative error of at most 0.004.
Values may be sent and summed in bfloat16 or wider, within the bound.
No kernel may reach another device: no remote copies, remote signals or barrier semaphores. Data moves between devices by JAX's collectives and lax.ppermute only.
A program may use at most 320 MiB of HBM per device.

```python
import math
import jax
import jax.numpy as jnp
from jax import lax

BLOCK_DOF = 320
OBJECTIVES = 512
INSTANCES = 8
COUPLE = 2
BLOCKS_DEV = 8
IFACE = 4
PARTITIONS = 8
BLOCKS = 64


def plant(drawn, stream_key, least, top_value):
    place = [jax.random.randint(jax.random.fold_in(stream_key, axis), (), 0, length) for axis, length in enumerate(drawn.shape)]
    widest = drawn.shape.index(max(drawn.shape))
    beside = place[:widest] + [(place[widest] + 1) % drawn.shape[widest]] + place[widest + 1:]
    return drawn.at[tuple(place)].set(least).at[tuple(beside)].set(top_value)


def steps_of(rng, extent, split, low, top_value):
    def one(dim, blocks):
        heights = jax.random.uniform(jax.random.fold_in(jax.random.fold_in(rng, 6), dim), (blocks,), jnp.float32, low / len(split), top_value / len(split))
        return jnp.repeat(jnp.exp(heights), extent[dim] // blocks).reshape((-1,) + (1,) * (len(extent) - dim - 1))

    loudness = one(*split[0])
    for cut in split[1:]:
        loudness = loudness * one(*cut)
    return loudness


def noise(key, shape, scale, reach, split=(), kind=jnp.bfloat16):
    entries = scale * jax.random.normal(key, shape, jnp.float32)
    if split:
        entries = entries * steps_of(key, shape, split, -0.22, 0.18)
    return jnp.clip(entries, -reach, reach).astype(kind)


def setup_inputs(seed: int = 0) -> dict:
    keys = jax.random.split(jax.random.key(seed), 9)
    return {
        "adjoint": noise(keys[0], (INSTANCES, BLOCKS, BLOCK_DOF, OBJECTIVES), 1.0, 6.0, ((0, 4), (1, 8))),
        "jacobian_diag": noise(keys[1], (INSTANCES, BLOCKS, BLOCK_DOF, BLOCK_DOF), BLOCK_DOF ** -0.5, 0.3125, ((0, 4), (1, 8))),
        "jacobian_off": noise(keys[2], (INSTANCES, BLOCKS, COUPLE, BLOCK_DOF, BLOCK_DOF), BLOCK_DOF ** -0.5, 0.3125, ((0, 4), (1, 8))),
        "off_columns": plant(jax.random.randint(keys[3], (BLOCKS, COUPLE), 0, BLOCKS_DEV + 2 * IFACE), jax.random.fold_in(keys[3], 1), 0, (BLOCKS_DEV + 2 * IFACE) - 1).astype(jnp.int32),
        "left_faces": plant(jax.random.randint(keys[4], (PARTITIONS, IFACE), 0, BLOCKS_DEV), jax.random.fold_in(keys[4], 1), 0, BLOCKS_DEV - 1).astype(jnp.int32),
        "right_faces": plant(jax.random.randint(keys[5], (PARTITIONS, IFACE), 0, BLOCKS_DEV), jax.random.fold_in(keys[5], 1), 0, BLOCKS_DEV - 1).astype(jnp.int32),
        "objective_grad": noise(keys[6], (INSTANCES, BLOCKS, BLOCK_DOF, OBJECTIVES), 1.0, 6.0, ((0, 4), (1, 8))),
        "pseudo_step": jnp.clip(jnp.exp(math.log(0.3) - 1.7917595 * jax.random.uniform(keys[7], (INSTANCES, BLOCKS, BLOCK_DOF), jnp.float32) ** steps_of(keys[7], (INSTANCES, BLOCKS, BLOCK_DOF), ((0, 4), (1, 8)), -0.2, 0.2)), 0.05, 0.3),
    }


def time_table(count):
    table = []
    for first in range(count):
        row_values = []
        for second in range(count):
            if first != second:
                delta = first - second
                parity = 1.0 - 2.0 * (delta % 2)
                row_values.append(0.5 * parity / math.tan(math.pi * delta / count))
            else:
                row_values.append(0.0)
        table.append(row_values)
    return table


def reference(adjoint, jacobian_diag, jacobian_off, off_columns, left_faces, right_faces, objective_grad, pseudo_step):
    highest = lax.Precision.HIGHEST
    table = jnp.asarray(time_table(INSTANCES), dtype=jnp.float32)
    owner = (jnp.arange(BLOCKS) // BLOCKS_DEV).astype(jnp.int32)
    before = ((owner - 1) % PARTITIONS).astype(jnp.int32)
    after = ((owner + 1) % PARTITIONS).astype(jnp.int32)
    targets = []
    for slot in range(COUPLE):
        code = off_columns[:, slot]
        left_slot = jnp.clip(code - BLOCKS_DEV, 0, IFACE - 1).astype(jnp.int32)
        right_slot = jnp.clip(code - BLOCKS_DEV - IFACE, 0, IFACE - 1).astype(jnp.int32)
        target = jnp.where(code < BLOCKS_DEV, owner * BLOCKS_DEV + code,
                           jnp.where(code < BLOCKS_DEV + IFACE,
                                     before * BLOCKS_DEV + right_faces[before, left_slot],
                                     after * BLOCKS_DEV + left_faces[after, right_slot]))
        targets.append(target.astype(jnp.int32))
    states = adjoint.astype(jnp.float32)
    outputs = []
    for inst in range(INSTANCES):
        state = states[inst]
        total = jnp.einsum("rbc,rbo->rco", jacobian_diag[inst].astype(jnp.float32), state, precision=highest)
        for slot in range(COUPLE):
            terms = jnp.einsum("rbc,rbo->rco", jacobian_off[inst, :, slot].astype(jnp.float32), state, precision=highest)
            rounded = lax.optimization_barrier(terms.astype(jnp.bfloat16))
            total = total + jax.ops.segment_sum(rounded.astype(jnp.float32), targets[slot], num_segments=BLOCKS)
        spectral = jnp.zeros_like(state)
        for other in range(INSTANCES):
            spectral = spectral + table[other, inst] * states[other]
        residual = total + spectral - objective_grad[inst].astype(jnp.float32)
        outputs.append((state - pseudo_step[inst][:, :, None] * residual).astype(jnp.bfloat16))
    return jnp.stack(outputs, 0)
```

```python
import functools
import math

import jax
import jax.numpy as jnp
from jax import lax
from jax.experimental import pallas as pl
from jax.experimental.pallas import tpu as pltpu
from jax.sharding import PartitionSpec as P


ANY = pl.BlockSpec(memory_space=pl.ANY)
SMEM = pl.BlockSpec(memory_space=pltpu.SMEM)
SLOTS = 3


def time_table(count):
    table = []
    for first in range(count):
        row_values = []
        for second in range(count):
            if first != second:
                delta = first - second
                parity = 1.0 - 2.0 * (delta % 2)
                row_values.append(0.5 * parity / math.tan(math.pi * delta / count))
            else:
                row_values.append(0.0)
        table.append(row_values)
    return table


def transposed_product(jacobian, state):
    return lax.dot_general(
        jacobian, state, (((0,), (0,)), ((), ())), preferred_element_type=jnp.float32
    )


def remote_kernel(inst, low, high, pieces, first, codes, state_hbm, off_hbm, *rest):
    outs, rest = rest[: len(pieces)], rest[len(pieces) :]
    if first:
        passed_hbm, *rest = rest
        *rest, passed, read_sem, write_sem = rest
    acc, states, jacobians, picked, state_sem, off_sem = rest
    blocks = codes.shape[1]

    def scan(term, found):
        code = codes[lax.div(term, blocks), lax.rem(term, blocks)]
        picked[found] = term
        return found + jnp.where((code >= low) & (code < high), 1, 0)

    found = lax.fori_loop(0, codes.shape[0] * blocks, scan, jnp.int32(0))

    def copies(index):
        slot = lax.rem(index, SLOTS)
        term = picked[index]
        row = lax.rem(term, blocks)
        return (
            pltpu.make_async_copy(state_hbm.at[inst, row], states.at[slot], state_sem.at[slot]),
            pltpu.make_async_copy(
                off_hbm.at[inst, row, lax.div(term, blocks)], jacobians.at[slot], off_sem.at[slot]
            ),
        )

    for ahead in range(SLOTS - 1):

        @pl.when(ahead < found)
        def _():
            for copy in copies(jnp.int32(ahead)):
                copy.start()

    if first:
        source = state_hbm.at[:, pl.ds(0, first)]
        pltpu.make_async_copy(source, passed, read_sem).start()
    acc[...] = jnp.zeros_like(acc)

    def one(index, carry):
        @pl.when(index + SLOTS - 1 < found)
        def _():
            for copy in copies(index + SLOTS - 1):
                copy.start()

        for copy in copies(index):
            copy.wait()
        slot = lax.rem(index, SLOTS)
        term = transposed_product(jacobians[slot], states[slot]).astype(jnp.bfloat16)
        chosen = picked[index]
        place = codes[lax.div(chosen, blocks), lax.rem(chosen, blocks)] - low
        acc[place] += term.astype(jnp.float32)
        return carry

    lax.fori_loop(0, found, one, 0)
    if first:
        pltpu.make_async_copy(source, passed, read_sem).wait()
        write = pltpu.make_async_copy(passed, passed_hbm, write_sem)
        write.start()
    for out, (slot_low, slot_high, row_low, row_high) in zip(outs, pieces):
        for slot in range(slot_low, slot_high):
            out[0, slot - slot_low] = acc[slot, row_low:row_high].astype(jnp.bfloat16)
    if first:
        write.wait()


def remote_terms(inst, low, high, pieces, codes, adjoint, off, first=0):
    insts, blocks, dof, wide = adjoint.shape
    couple = off.shape[2]
    shapes = [
        jax.ShapeDtypeStruct((1, b - a, d - c, wide), jnp.bfloat16) for a, b, c, d in pieces
    ]
    out_specs = [pl.BlockSpec(memory_space=pltpu.VMEM)] * len(pieces)
    extra = []
    if first:
        passed = (insts, first, dof, wide)
        shapes.append(jax.ShapeDtypeStruct(passed, jnp.bfloat16))
        out_specs.append(ANY)
        extra = [
            pltpu.VMEM(passed, jnp.bfloat16),
            pltpu.SemaphoreType.DMA(()),
            pltpu.SemaphoreType.DMA(()),
        ]
    work = high - low
    return pl.pallas_call(
        functools.partial(remote_kernel, inst, low, high, pieces, first),
        out_shape=shapes,
        in_specs=[SMEM, ANY, ANY],
        out_specs=out_specs,
        scratch_shapes=[
            pltpu.VMEM((high - low, dof, wide), jnp.float32),
            pltpu.VMEM((SLOTS, dof, wide), jnp.bfloat16),
            pltpu.VMEM((SLOTS, dof, dof), jnp.bfloat16),
            pltpu.SMEM((couple * blocks + 1,), jnp.int32),
            pltpu.SemaphoreType.DMA((SLOTS,)),
            pltpu.SemaphoreType.DMA((SLOTS,)),
            *extra,
        ],
        cost_estimate=pl.CostEstimate(
            flops=2 * work * dof * dof * wide,
            bytes_accessed=work * 2 * dof * (dof + wide),
            transcendentals=0,
        ),
    )(codes, adjoint, off)


def local_kernel(
    insts, couple, first, codes, here, table, adj_all, near_all, far_all, relay_all,
    state, diag, off, grad, step, base, acc,
):
    inst, row = pl.program_id(0), pl.program_id(1)
    blocks = pl.num_programs(1)

    @pl.when(row == 0)
    def _():
        acc[...] = jnp.zeros_like(acc)

    acc[row] += transposed_product(diag[0, 0], state[0, 0])
    for slot in range(couple):
        code = codes[slot, row]

        @pl.when(code < blocks)
        def _():
            term = transposed_product(off[0, 0, slot], state[0, 0]).astype(jnp.bfloat16)
            acc[code] += term.astype(jnp.float32)

    @pl.when(row == blocks - 1)
    def _():
        def mix(total, block, sources, at):
            for index, source in enumerate(sources):
                for other in range(insts):
                    sender = here[0] ^ (at + index)
                    weight = table[sender * insts + other, here[0] * insts + inst]
                    total += weight * source[other, block].astype(jnp.float32)
            return total

        def finish(block, carry):
            total = acc[block] - grad[0, block].astype(jnp.float32)
            total = mix(total, block, (adj_all, near_all), 0)
            mine = adj_all[inst, block].astype(jnp.float32)
            base[0, block] = mine - step[0, block] * total
            return carry

        def finish_far(block, carry):
            total = mix(jnp.zeros(acc.shape[1:], jnp.float32), block, (far_all, relay_all), 2)
            base[0, block] -= step[0, block] * total
            return carry

        lax.fori_loop(0, base.shape[1], finish, 0)
        lax.fori_loop(0, first, finish_far, 0)


def local_part(codes, here, table, adjoint, near, far, relay, diag, off, grad, step):
    insts, blocks, dof, wide = adjoint.shape
    couple = off.shape[2]
    first = far.shape[1]

    def whole(shape):
        return pl.BlockSpec(shape, lambda n, r: (0, 0, 0, 0), pipeline_mode=pl.Buffered(1))

    return pl.pallas_call(
        functools.partial(local_kernel, insts, couple, first),
        grid=(insts, blocks),
        out_shape=jax.ShapeDtypeStruct(adjoint.shape, jnp.float32),
        in_specs=[
            SMEM,
            SMEM,
            SMEM,
            whole(adjoint.shape),
            whole(near.shape),
            whole(far.shape),
            whole(relay.shape),
            pl.BlockSpec((1, 1, dof, wide), lambda n, r: (n, r, 0, 0)),
            pl.BlockSpec((1, 1, dof, dof), lambda n, r: (n, r, 0, 0)),
            pl.BlockSpec((1, 1, couple, dof, dof), lambda n, r: (n, r, 0, 0, 0)),
            pl.BlockSpec((1, blocks, dof, wide), lambda n, r: (n, 0, 0, 0)),
            pl.BlockSpec((1, blocks, dof, 1), lambda n, r: (n, 0, 0, 0)),
        ],
        out_specs=pl.BlockSpec((1, blocks, dof, wide), lambda n, r: (n, 0, 0, 0)),
        scratch_shapes=[pltpu.VMEM((blocks, dof, wide), jnp.float32)],
        cost_estimate=pl.CostEstimate(
            flops=4 * insts * blocks * dof * dof * wide,
            bytes_accessed=insts * blocks * dof * (6 * dof + 12 * wide),
            transcendentals=0,
        ),
        name="local_part",
    )(codes, here, table, adjoint, near, far, relay, adjoint, diag, off, grad, step)


def mix_kernel(insts, pieces, here, table, own, near, *outs):
    for inst in range(insts):
        total = None
        for index, source in enumerate((own, near)):
            for other in range(insts):
                sender, target = here[0] ^ index, here[0] ^ 2
                weight = table[sender * insts + other, target * insts + inst]
                term = weight * source[other, 0].astype(jnp.float32)
                total = term if total is None else total + term
        total = total.astype(jnp.bfloat16)
        for out, (which, low, high) in zip(outs, pieces):
            if which == inst:
                out[0, 0] = total[low:high]


def mix(here, table, adjoint, near, first, pieces):
    insts, blocks, dof, wide = adjoint.shape
    state = pl.BlockSpec((insts, 1, dof, wide), lambda r: (0, r + first, 0, 0))
    count = blocks - first
    return pl.pallas_call(
        functools.partial(mix_kernel, insts, pieces),
        grid=(count,),
        out_shape=[
            jax.ShapeDtypeStruct((1, count, high - low, wide), jnp.bfloat16)
            for _, low, high in pieces
        ],
        in_specs=[SMEM, SMEM, state, state],
        out_specs=[
            pl.BlockSpec((1, 1, high - low, wide), lambda r: (0, r, 0, 0))
            for _, low, high in pieces
        ],
        cost_estimate=pl.CostEstimate(
            flops=8 * insts * count * dof * wide,
            bytes_accessed=6 * insts * count * dof * wide,
            transcendentals=0,
        ),
        name="mix",
    )(here, table, adjoint, near)


def final_kernel(group, first, places, left, right, base, step, far, *rest):
    arrivals = rest[: len(places)]
    out, total = rest[-2:]
    start = pl.program_id(0) * group

    def one(inner, carry):
        block = start + inner
        known = far[0, jnp.maximum(block - first, 0)]
        total[...] = jnp.where(block >= first, known, 0).astype(jnp.float32)
        for arrived, (side, offset) in zip(arrivals, places):
            faces = (left, right)[side]
            for slot in range(arrived.shape[1]):

                @pl.when(faces[0, offset + slot] == block)
                def _():
                    total[...] += arrived[0, slot].astype(jnp.float32)

        out[0, inner] = (base[0, inner] - step[0, inner] * total[...]).astype(jnp.bfloat16)
        return carry

    lax.fori_loop(0, group, one, 0)


def final_part(inst, row_low, row_high, group, left, right, base, step, far, arrivals, out, limit):
    _, blocks, _, wide = base.shape
    rows = row_high - row_low
    at = row_low // rows
    state = pl.BlockSpec((1, group, rows, wide), lambda g: (inst, g, at, 0))
    whole = lambda x: pl.BlockSpec(x.shape, lambda g: (0, 0, 0, 0), pipeline_mode=pl.Buffered(1))
    terms = [x for _, _, x in arrivals]
    places = [(side, offset) for side, offset, _ in arrivals]
    operands = [left, right, base, step, far, *terms]
    specs = [
        SMEM,
        SMEM,
        state,
        pl.BlockSpec((1, group, rows, 1), lambda g: (inst, g, at, 0)),
        whole(far),
        *[whole(x) for x in terms],
    ]
    aliases = {}
    if out is not None:
        aliases = {len(operands): 0}
        operands.append(out)
        specs.append(ANY)
    return pl.pallas_call(
        functools.partial(final_kernel, group, blocks - far.shape[1], places),
        grid=(blocks // group,),
        out_shape=jax.ShapeDtypeStruct(base.shape, jnp.bfloat16),
        in_specs=specs,
        out_specs=state,
        scratch_shapes=[pltpu.VMEM((rows, wide), jnp.float32)],
        input_output_aliases=aliases,
        cost_estimate=pl.CostEstimate(
            flops=20 * blocks * rows * wide,
            bytes_accessed=10 * blocks * rows * wide,
            transcendentals=0,
        ),
        compiler_params=pltpu.CompilerParams(vmem_limit_bytes=limit << 20),
    )(*operands)


def per_device(adjoint, diag, off, off_columns, left, right, grad, step):
    insts, blocks, dof, _ = adjoint.shape
    iface = left.shape[1]
    parts, times = lax.axis_size("space"), lax.axis_size("tm")
    if times != 4 or insts != 2:
        raise ValueError("unsupported tm size")
    instances = insts * times
    here = lax.axis_index("tm").astype(jnp.int32)[None]
    table = jnp.asarray(time_table(instances), dtype=jnp.float32)
    swap_core = [(i, i ^ 1) for i in range(times)]
    swap_chip = [(i, i ^ 2) for i in range(times)]
    up = [(i, (i + 1) % parts) for i in range(parts)]
    down = [(j, i) for i, j in up]
    codes = off_columns.T

    cut, first, ends = 256, 2, blocks + 2 * iface

    half = iface // 2
    up0, passed = remote_terms(
        0, ends - half, ends, [(0, half, 0, dof)], codes, adjoint, off, first
    )
    before0 = lax.ppermute(up0, "space", up)
    far0 = lax.ppermute(passed, "tm", swap_chip)
    near = lax.ppermute(adjoint, "tm", swap_core)
    pieces = [(iface, 2 * iface - half, 0, dof), (0, iface, 0, dof)]
    up0b, down0 = remote_terms(0, blocks, ends - half, pieces, codes, adjoint, off)
    before0b = lax.ppermute(up0b, "space", up)
    after0 = lax.ppermute(down0, "space", down)
    pieces = [
        (iface, 2 * iface, 0, cut),
        (0, iface, 0, cut),
        (iface, 2 * iface, cut, dof),
        (0, iface, cut, dof),
    ]
    up1a, down1a, up1b, down1b = remote_terms(1, blocks, ends, pieces, codes, adjoint, off)
    mixed = mix(here, table, adjoint, near, first, [(0, 0, dof), (1, 0, cut), (1, cut, dof)])
    far1 = lax.ppermute(mixed[0], "tm", swap_chip)
    far2a = lax.ppermute(mixed[1], "tm", swap_chip)
    far2b = lax.ppermute(mixed[2], "tm", swap_chip)
    before1a = lax.ppermute(up1a, "space", up)
    after1a = lax.ppermute(down1a, "space", down)
    before1b = lax.ppermute(up1b, "space", up)
    after1b = lax.ppermute(down1b, "space", down)
    relay = lax.ppermute(far0, "tm", swap_core)
    step = step[..., None]
    base = local_part(codes, here, table, adjoint, near, far0, relay, diag, off, grad, step)
    arrivals = [(0, iface - half, before0), (0, 0, before0b), (1, 0, after0)]
    out = final_part(0, 0, dof, 1, left, right, base, step, far1, arrivals, None, 16)
    arrivals = [(0, 0, before1a), (1, 0, after1a)]
    out = final_part(1, 0, cut, 1, left, right, base, step, far2a, arrivals, out, 16)
    arrivals = [(0, 0, before1b), (1, 0, after1b)]
    return final_part(1, cut, dof, blocks, left, right, base, step, far2b, arrivals, out, 12)


def solution(mesh):
    in_specs = (
        P("tm", "space", None, None),
        P("tm", "space", None, None),
        P("tm", "space", None, None, None),
        P("space", None),
        P("space", None),
        P("space", None),
        P("tm", "space", None, None),
        P("tm", "space", None),
    )
    out_specs = P("tm", "space", None, None)
    return jax.shard_map(
        per_device, mesh=mesh, in_specs=in_specs, out_specs=out_specs, check_vma=False
    )
```

```python
import functools
import math

import jax
import jax.numpy as jnp
from jax import lax
from jax.experimental import pallas as pl
from jax.experimental.pallas import tpu as pltpu
from jax.sharding import PartitionSpec as P


ANY = pl.BlockSpec(memory_space=pl.ANY)
SMEM = pl.BlockSpec(memory_space=pltpu.SMEM)
SLOTS = 3


def time_table(count):
    table = []
    for first in range(count):
        row_values = []
        for second in range(count):
            if first != second:
                delta = first - second
                parity = 1.0 - 2.0 * (delta % 2)
                row_values.append(0.5 * parity / math.tan(math.pi * delta / count))
            else:
                row_values.append(0.0)
        table.append(row_values)
    return table


def transposed_product(jacobian, state):
    return lax.dot_general(
        jacobian, state, (((0,), (0,)), ((), ())), preferred_element_type=jnp.float32
    )


def parity():
    return lax.rem(lax.axis_index("space"), 2)


def remote_kernel(inst, iface, ranges, pieces, first, codes_hbm, state_hbm, off_hbm, *rest):
    outs, rest = rest[: len(pieces)], rest[len(pieces) :]
    if first:
        passed_hbm, *rest = rest
        *rest, passed, read_sem, write_sem = rest
    codes, code_sem, acc, states, jacobians, picked, places, *rest = rest
    state_sem, off_sem, ready, out_sem = rest
    load_codes = pltpu.make_async_copy(codes_hbm, codes, code_sem)
    load_codes.start()
    if first:
        source = state_hbm.at[:, pl.ds(0, first)]
        pltpu.make_async_copy(source, passed, read_sem).start()
    blocks = codes.shape[1]
    odd = parity()
    lows = (blocks + iface * (1 - odd), blocks + iface * odd)
    acc[...] = jnp.zeros_like(acc)
    load_codes.wait()

    def scan(term, found):
        code = codes[lax.div(term, blocks), lax.rem(term, blocks)]
        hits, place, base = 0, 0, 0
        for kind, offset, count in ranges:
            at = code - (lows[kind] + offset)
            inside = (at >= 0) & (at < count)
            place = jnp.where(inside, at + base, place)
            hits = jnp.where(inside, 1, hits)
            base += count
        picked[found] = term
        places[found] = place
        return found + hits

    found = lax.fori_loop(0, codes.shape[0] * blocks, scan, jnp.int32(0))

    def copies(index):
        slot = lax.rem(index, SLOTS)
        term = picked[index]
        row = lax.rem(term, blocks)
        return (
            pltpu.make_async_copy(state_hbm.at[inst, row], states.at[slot], state_sem.at[slot]),
            pltpu.make_async_copy(
                off_hbm.at[inst, row, lax.div(term, blocks)], jacobians.at[slot], off_sem.at[slot]
            ),
        )

    for ahead in range(SLOTS - 1):

        @pl.when(ahead < found)
        def _():
            for copy in copies(jnp.int32(ahead)):
                copy.start()

    def one(index, carry):
        @pl.when(index + SLOTS - 1 < found)
        def _():
            for copy in copies(index + SLOTS - 1):
                copy.start()

        for copy in copies(index):
            copy.wait()
        slot = lax.rem(index, SLOTS)
        term = transposed_product(jacobians[slot], states[slot]).astype(jnp.bfloat16)
        acc[places[index]] += term.astype(jnp.float32)
        return carry

    if first:
        pltpu.make_async_copy(source, passed, read_sem).wait()
        write = pltpu.make_async_copy(passed, passed_hbm, write_sem)
        write.start()
    lax.fori_loop(0, found, one, 0)
    writes = []
    for slot in range(acc.shape[0]):
        ready[slot] = acc[slot].astype(jnp.bfloat16)
        for out, (slot_low, slot_high, row_low, row_high) in zip(outs, pieces):
            if slot_low <= slot < slot_high:
                piece = ready.at[slot, pl.ds(row_low, row_high - row_low)]
                copy = pltpu.make_async_copy(
                    piece, out.at[0, slot - slot_low], out_sem.at[len(writes)]
                )
                copy.start()
                writes.append(copy)
    for copy in writes:
        copy.wait()
    if first:
        write.wait()


def remote_terms(inst, iface, ranges, pieces, codes, adjoint, off, first=0):
    insts, blocks, dof, wide = adjoint.shape
    couple = off.shape[2]
    shapes = [
        jax.ShapeDtypeStruct((1, b - a, d - c, wide), jnp.bfloat16) for a, b, c, d in pieces
    ]
    out_specs = [ANY] * len(pieces)
    extra = []
    if first:
        passed = (insts, first, dof, wide)
        shapes.append(jax.ShapeDtypeStruct(passed, jnp.bfloat16))
        out_specs.append(ANY)
        extra = [
            pltpu.VMEM(passed, jnp.bfloat16),
            pltpu.SemaphoreType.DMA(()),
            pltpu.SemaphoreType.DMA(()),
        ]
    work = sum(count for _, _, count in ranges)
    return pl.pallas_call(
        functools.partial(remote_kernel, inst, iface, ranges, pieces, first),
        out_shape=shapes,
        in_specs=[ANY, ANY, ANY],
        out_specs=out_specs,
        scratch_shapes=[
            pltpu.SMEM((couple, blocks), jnp.int32),
            pltpu.SemaphoreType.DMA(()),
            pltpu.VMEM((work, dof, wide), jnp.float32),
            pltpu.VMEM((SLOTS, dof, wide), jnp.bfloat16),
            pltpu.VMEM((SLOTS, dof, dof), jnp.bfloat16),
            pltpu.SMEM((couple * blocks + 1,), jnp.int32),
            pltpu.SMEM((couple * blocks + 1,), jnp.int32),
            pltpu.SemaphoreType.DMA((SLOTS,)),
            pltpu.SemaphoreType.DMA((SLOTS,)),
            pltpu.VMEM((work, dof, wide), jnp.bfloat16),
            pltpu.SemaphoreType.DMA((sum(b - a for a, b, _, _ in pieces),)),
            *extra,
        ],
        cost_estimate=pl.CostEstimate(
            flops=2 * work * dof * dof * wide,
            bytes_accessed=work * 2 * dof * (dof + wide),
            transcendentals=0,
        ),
    )(codes, adjoint, off)


def local_kernel(
    inst, insts, couple, first, codes, here, table, left, right, adj_all, near_all, far_all,
    relay_all, arrived, state, diag, off, grad, step, base, acc,
):
    row = pl.program_id(0)
    blocks = pl.num_programs(0)

    @pl.when(row == 0)
    def _():
        acc[...] = jnp.zeros_like(acc)

    acc[row] += transposed_product(diag[0, 0], state[0, 0])
    for slot in range(couple):
        code = codes[slot, row]

        @pl.when(code < blocks)
        def _():
            term = transposed_product(off[0, 0, slot], state[0, 0]).astype(jnp.bfloat16)
            acc[code] += term.astype(jnp.float32)

    @pl.when(row == blocks - 1)
    def _():
        odd = parity()
        for slot in range(arrived.shape[1]):
            block = jnp.where(odd == 0, left[0, slot], right[0, slot])
            acc[block] += arrived[0, slot].astype(jnp.float32)

        def mix(total, block, sources, at):
            for index, source in enumerate(sources):
                for other in range(insts):
                    sender = here[0] ^ (at + index)
                    weight = table[sender * insts + other, here[0] * insts + inst]
                    total += weight * source[other, block].astype(jnp.float32)
            return total

        def finish(block, carry):
            total = acc[block] - grad[0, block].astype(jnp.float32)
            total = mix(total, block, (adj_all, near_all), 0)
            mine = adj_all[inst, block].astype(jnp.float32)
            base[0, block] = mine - step[0, block] * total
            return carry

        def finish_far(block, carry):
            total = mix(jnp.zeros(acc.shape[1:], jnp.float32), block, (far_all, relay_all), 2)
            base[0, block] -= step[0, block] * total
            return carry

        lax.fori_loop(0, base.shape[1], finish, 0)
        lax.fori_loop(0, first, finish_far, 0)


def local_part(
    inst, codes, here, table, left, right, adjoint, near, far, relay, arrived, diag, off, grad, step
):
    insts, blocks, dof, wide = adjoint.shape
    couple = off.shape[2]
    first = far.shape[1]

    def whole(x):
        return pl.BlockSpec(x.shape, lambda r: (0, 0, 0, 0), pipeline_mode=pl.Buffered(1))

    return pl.pallas_call(
        functools.partial(local_kernel, inst, insts, couple, first),
        grid=(blocks,),
        out_shape=jax.ShapeDtypeStruct((1, blocks, dof, wide), jnp.float32),
        in_specs=[
            SMEM,
            SMEM,
            SMEM,
            SMEM,
            SMEM,
            whole(adjoint),
            whole(near),
            whole(far),
            whole(relay),
            whole(arrived),
            pl.BlockSpec((1, 1, dof, wide), lambda r: (inst, r, 0, 0)),
            pl.BlockSpec((1, 1, dof, dof), lambda r: (inst, r, 0, 0)),
            pl.BlockSpec((1, 1, couple, dof, dof), lambda r: (inst, r, 0, 0, 0)),
            pl.BlockSpec((1, blocks, dof, wide), lambda r: (inst, 0, 0, 0)),
            pl.BlockSpec((1, blocks, dof, 1), lambda r: (inst, 0, 0, 0)),
        ],
        out_specs=pl.BlockSpec((1, blocks, dof, wide), lambda r: (0, 0, 0, 0)),
        scratch_shapes=[pltpu.VMEM((blocks, dof, wide), jnp.float32)],
        cost_estimate=pl.CostEstimate(
            flops=4 * blocks * dof * dof * wide,
            bytes_accessed=blocks * dof * (6 * dof + 12 * wide),
            transcendentals=0,
        ),
    )(
        codes, here, table, left, right, adjoint, near, far, relay, arrived, adjoint, diag, off,
        grad, step,
    )


def mix_kernel(insts, pieces, here, table, own, near, *outs):
    for inst in range(insts):
        total = None
        for index, source in enumerate((own, near)):
            for other in range(insts):
                sender, target = here[0] ^ index, here[0] ^ 2
                weight = table[sender * insts + other, target * insts + inst]
                term = weight * source[other, 0].astype(jnp.float32)
                total = term if total is None else total + term
        total = total.astype(jnp.bfloat16)
        for out, (which, low, high) in zip(outs, pieces):
            if which == inst:
                out[0, 0] = total[low:high]


def mix(here, table, adjoint, near, first, pieces):
    insts, blocks, dof, wide = adjoint.shape
    state = pl.BlockSpec((insts, 1, dof, wide), lambda r: (0, r + first, 0, 0))
    count = blocks - first
    return pl.pallas_call(
        functools.partial(mix_kernel, insts, pieces),
        grid=(count,),
        out_shape=[
            jax.ShapeDtypeStruct((1, count, high - low, wide), jnp.bfloat16)
            for _, low, high in pieces
        ],
        in_specs=[SMEM, SMEM, state, state],
        out_specs=[
            pl.BlockSpec((1, 1, high - low, wide), lambda r: (0, r, 0, 0))
            for _, low, high in pieces
        ],
        cost_estimate=pl.CostEstimate(
            flops=8 * insts * count * dof * wide,
            bytes_accessed=6 * insts * count * dof * wide,
            transcendentals=0,
        ),
        name="mix",
    )(here, table, adjoint, near)


def final_kernel(where, group, first, offsets, left, right, base, step, far, *rest):
    arrivals = rest[: len(offsets)]
    if where is None:
        out, total = rest[-2:]
    else:
        out_hbm, total, out, out_sem = rest[-4:]
        inst, row_low, rows = where
    start = pl.program_id(0) * group
    odd = parity()
    slots = [(x, s, offset + s) for x, offset in zip(arrivals, offsets) for s in range(x.shape[1])]

    def one(inner, carry):
        block = start + inner
        place = 0 if group == 1 else jnp.maximum(block - first, 0)
        chosen = [jnp.where(odd == 0, right[0, s], left[0, s]) == block for _, _, s in slots]
        touched = functools.reduce(jnp.logical_or, chosen)
        late = block >= first

        def put(value):
            out[0, inner] = (base[0, inner] - step[0, inner] * value).astype(jnp.bfloat16)

        @pl.when(late & ~touched)
        def _():
            put(far[0, place].astype(jnp.float32))

        @pl.when(~late & ~touched)
        def _():
            out[0, inner] = base[0, inner].astype(jnp.bfloat16)

        @pl.when(touched)
        def _():
            total[...] = jnp.where(late, far[0, place].astype(jnp.float32), 0.0)
            for (arrived, slot, _), hit in zip(slots, chosen):

                @pl.when(hit)
                def _():
                    total[...] += arrived[0, slot].astype(jnp.float32)

            put(total[...])

        if where is not None:
            write(block).start()
        return carry

    def write(block):
        target = out_hbm.at[inst, block, pl.ds(row_low, rows)]
        return pltpu.make_async_copy(out.at[0, block], target, out_sem.at[block])

    lax.fori_loop(0, group, one, 0)
    if where is not None:
        for block in range(group):
            write(block).wait()


def final_part(inst, row_low, row_high, group, left, right, base, step, far, arrivals, out, limit):
    insts = step.shape[0]
    _, blocks, dof, wide = base.shape
    rows = row_high - row_low
    at = row_low // rows
    first = blocks - far.shape[1]
    state = pl.BlockSpec((1, group, rows, wide), lambda g: (inst, g, at, 0))
    whole = lambda x: pl.BlockSpec(x.shape, lambda g: (0, 0, 0, 0), pipeline_mode=pl.Buffered(1))
    terms = [x for _, x in arrivals]
    operands = [left, right, base, step, far, *terms]
    specs = [
        SMEM,
        SMEM,
        pl.BlockSpec((1, group, rows, wide), lambda g: (0, g, at, 0)),
        pl.BlockSpec((1, group, rows, 1), lambda g: (inst, g, at, 0)),
        whole(far)
        if group > 1
        else pl.BlockSpec((1, 1, rows, wide), lambda g: (0, jnp.maximum(g - first, 0), 0, 0)),
        *[whole(x) for x in terms],
    ]
    last = group == blocks
    scratch = [pltpu.VMEM((rows, wide), jnp.float32)]
    if last:
        scratch.append(pltpu.VMEM((1, blocks, rows, wide), jnp.bfloat16))
        scratch.append(pltpu.SemaphoreType.DMA((blocks,)))
    aliases = {}
    if out is not None:
        aliases = {len(operands): 0}
        operands.append(out)
        specs.append(ANY)
    return pl.pallas_call(
        functools.partial(
            final_kernel,
            (inst, row_low, rows) if last else None,
            group,
            first,
            [offset for offset, _ in arrivals],
        ),
        grid=(blocks // group,),
        out_shape=jax.ShapeDtypeStruct((insts, blocks, dof, wide), jnp.bfloat16),
        in_specs=specs,
        out_specs=ANY if last else state,
        scratch_shapes=scratch,
        input_output_aliases=aliases,
        cost_estimate=pl.CostEstimate(
            flops=20 * blocks * rows * wide,
            bytes_accessed=10 * blocks * rows * wide,
            transcendentals=0,
        ),
        compiler_params=pltpu.CompilerParams(vmem_limit_bytes=limit << 20),
    )(*operands)


def per_device(adjoint, diag, off, off_columns, left, right, grad, step):
    insts, blocks, dof, _ = adjoint.shape
    iface = left.shape[1]
    parts, times = lax.axis_size("space"), lax.axis_size("tm")
    if times != 4 or insts != 2 or parts % 2:
        raise ValueError("unsupported mesh")
    instances = insts * times
    here = lax.axis_index("tm").astype(jnp.int32)[None]
    table = jnp.asarray(time_table(instances), dtype=jnp.float32)
    swap_core = [(i, i ^ 1) for i in range(times)]
    swap_chip = [(i, i ^ 2) for i in range(times)]
    pair = [(i, i ^ 1) for i in range(parts)]
    other = [(i, (i + 2 * (i % 2) - 1) % parts) for i in range(parts)]
    codes = off_columns.T
    cut, first, half = 256, 2, iface // 2

    ranges, pieces = [(0, half, iface - half)], [(0, iface - half, 0, dof)]
    pair0a, passed = remote_terms(0, iface, ranges, pieces, codes, adjoint, off, first)
    far0 = lax.ppermute(passed, "tm", swap_chip)
    from_pair0a = lax.ppermute(pair0a, "space", pair)
    near = lax.ppermute(adjoint, "tm", swap_core)
    ranges = [(1, 0, iface), (0, 0, half)]
    pieces = [(0, iface, 0, dof), (iface, iface + half, 0, dof)]
    other0, pair0b = remote_terms(0, iface, ranges, pieces, codes, adjoint, off)
    from_other0 = lax.ppermute(other0, "space", other)
    from_pair0b = lax.ppermute(pair0b, "space", pair)
    mixed = mix(here, table, adjoint, near, first, [(0, 0, dof), (1, 0, cut), (1, cut, dof)])
    far1 = lax.ppermute(mixed[0], "tm", swap_chip)
    far2a = lax.ppermute(mixed[1], "tm", swap_chip)
    far2b = lax.ppermute(mixed[2], "tm", swap_chip)
    ranges = [(1, 0, iface), (0, 0, iface)]
    pieces = [(0, iface, 0, dof), (iface, 2 * iface, 0, cut), (iface, 2 * iface, cut, dof)]
    other1, pair1a, pair1b = remote_terms(1, iface, ranges, pieces, codes, adjoint, off)
    from_other1 = lax.ppermute(other1, "space", other)
    from_pair1a = lax.ppermute(pair1a, "space", pair)
    from_pair1b = lax.ppermute(pair1b, "space", pair)
    relay = lax.ppermute(far0, "tm", swap_core)
    step = step[..., None]
    common = (codes, here, table, left, right, adjoint, near, far0, relay)
    base0 = local_part(0, *common, from_other0, diag, off, grad, step)
    base1 = local_part(1, *common, from_other1, diag, off, grad, step)
    faces = (left, right)
    arrivals = [(half, from_pair0a), (0, from_pair0b)]
    out = final_part(0, 0, dof, 2, *faces, base0, step, far1, arrivals, None, 16)
    out = final_part(1, 0, cut, 4, *faces, base1, step, far2a, [(0, from_pair1a)], out, 20)
    arrivals = [(0, from_pair1b)]
    return final_part(1, cut, dof, blocks, *faces, base1, step, far2b, arrivals, out, 12)


def solution(mesh):
    in_specs = (
        P("tm", "space", None, None),
        P("tm", "space", None, None),
        P("tm", "space", None, None, None),
        P("space", None),
        P("space", None),
        P("space", None),
        P("tm", "space", None, None),
        P("tm", "space", None),
    )
    out_specs = P("tm", "space", None, None)
    return jax.shard_map(
        per_device, mesh=mesh, in_specs=in_specs, out_specs=out_specs, check_vma=False
    )
```

```python
import functools
import math

import jax
import jax.numpy as jnp
from jax import lax
from jax.experimental import pallas as pl
from jax.experimental.pallas import tpu as pltpu
from jax.sharding import PartitionSpec as P


ANY = pl.BlockSpec(memory_space=pl.ANY)
SMEM = pl.BlockSpec(memory_space=pltpu.SMEM)
VMEM = pl.BlockSpec(memory_space=pltpu.VMEM)
SLOTS = 3
ROOM = 56 << 20
LOCAL_ROOM = 58 << 20


def time_table(count):
    table = []
    for first in range(count):
        row_values = []
        for second in range(count):
            if first != second:
                delta = first - second
                parity = 1.0 - 2.0 * (delta % 2)
                row_values.append(0.5 * parity / math.tan(math.pi * delta / count))
            else:
                row_values.append(0.0)
        table.append(row_values)
    return table


def transposed_product(jacobian, state):
    return lax.dot_general(
        jacobian, state, (((0,), (0,)), ((), ())), preferred_element_type=jnp.float32
    )


def parity():
    return lax.rem(lax.axis_index("space"), 2)


def remote_kernel(inst, iface, ranges, pieces, first, codes_hbm, state_hbm, off_hbm, *rest):
    outs, rest = rest[: len(pieces)], rest[len(pieces) :]
    if first:
        passed, *rest = rest
        *rest, read_sem = rest
    else:
        *rest, ready, out_sem = rest
    codes, code_sem, acc, states, jacobians, picked, places, state_sem, off_sem = rest
    load_codes = pltpu.make_async_copy(codes_hbm, codes, code_sem)
    load_codes.start()
    if first:
        source = state_hbm.at[:, pl.ds(0, first)]
        pltpu.make_async_copy(source, passed, read_sem).start()
    blocks = codes.shape[1]
    odd = parity()
    lows = (blocks + iface * (1 - odd), blocks + iface * odd)
    acc[...] = jnp.zeros_like(acc)
    load_codes.wait()

    found = jnp.int32(0)
    for term in range(codes.shape[0] * blocks):
        code = codes[term // blocks, term % blocks]
        hits, place, base = 0, 0, 0
        for kind, offset, count in ranges:
            at = code - (lows[kind] + offset)
            inside = (at >= 0) & (at < count)
            place = jnp.where(inside, at + base, place)
            hits = jnp.where(inside, 1, hits)
            base += count
        picked[found] = term
        places[found] = place
        found = found + hits

    def copies(index):
        slot = lax.rem(index, SLOTS)
        term = picked[index]
        row = lax.rem(term, blocks)
        return (
            pltpu.make_async_copy(state_hbm.at[inst, row], states.at[slot], state_sem.at[slot]),
            pltpu.make_async_copy(
                off_hbm.at[inst, row, lax.div(term, blocks)], jacobians.at[slot], off_sem.at[slot]
            ),
        )

    for ahead in range(SLOTS - 1):

        @pl.when(ahead < found)
        def _():
            for copy in copies(jnp.int32(ahead)):
                copy.start()

    def one(index, carry):
        @pl.when(index + SLOTS - 1 < found)
        def _():
            for copy in copies(index + SLOTS - 1):
                copy.start()

        for copy in copies(index):
            copy.wait()
        slot = lax.rem(index, SLOTS)
        term = transposed_product(jacobians[slot], states[slot]).astype(jnp.bfloat16)
        acc[places[index]] += term.astype(jnp.float32)
        return carry

    lax.fori_loop(0, found, one, 0)
    if first:
        for out, (slot_low, slot_high, row_low, row_high) in zip(outs, pieces):
            for slot in range(slot_low, slot_high):
                out[0, slot - slot_low] = acc[slot, row_low:row_high].astype(jnp.bfloat16)
        pltpu.make_async_copy(source, passed, read_sem).wait()
        return
    writes = []
    for slot in range(acc.shape[0]):
        ready[slot] = acc[slot].astype(jnp.bfloat16)
        for out, (slot_low, slot_high, row_low, row_high) in zip(outs, pieces):
            if slot_low <= slot < slot_high:
                piece = ready.at[slot, pl.ds(row_low, row_high - row_low)]
                copy = pltpu.make_async_copy(
                    piece, out.at[0, slot - slot_low], out_sem.at[len(writes)]
                )
                copy.start()
                writes.append(copy)
    for copy in writes:
        copy.wait()


def remote_terms(inst, iface, ranges, pieces, codes, adjoint, off, first=0):
    insts, blocks, dof, wide = adjoint.shape
    couple = off.shape[2]
    work = sum(count for _, _, count in ranges)
    shapes = [(1, b - a, d - c, wide) for a, b, c, d in pieces]
    if first:
        shapes.append((insts, first, dof, wide))
        shapes = [pltpu.VMEM(shape, jnp.bfloat16) for shape in shapes]
        out_specs = [VMEM] * len(shapes)
        extra = [pltpu.SemaphoreType.DMA(())]
    else:
        shapes = [jax.ShapeDtypeStruct(shape, jnp.bfloat16) for shape in shapes]
        out_specs = [ANY] * len(shapes)
        extra = [
            pltpu.VMEM((work, dof, wide), jnp.bfloat16),
            pltpu.SemaphoreType.DMA((sum(b - a for a, b, _, _ in pieces),)),
        ]
    return pl.pallas_call(
        functools.partial(remote_kernel, inst, iface, ranges, pieces, first),
        out_shape=shapes,
        in_specs=[ANY, ANY, ANY],
        out_specs=out_specs,
        scratch_shapes=[
            pltpu.SMEM((couple, blocks), jnp.int32),
            pltpu.SemaphoreType.DMA(()),
            pltpu.VMEM((work, dof, wide), jnp.float32),
            pltpu.VMEM((SLOTS, dof, wide), jnp.bfloat16),
            pltpu.VMEM((SLOTS, dof, dof), jnp.bfloat16),
            pltpu.SMEM((couple * blocks + 1,), jnp.int32),
            pltpu.SMEM((couple * blocks + 1,), jnp.int32),
            pltpu.SemaphoreType.DMA((SLOTS,)),
            pltpu.SemaphoreType.DMA((SLOTS,)),
            *extra,
        ],
        cost_estimate=pl.CostEstimate(
            flops=2 * work * dof * dof * wide,
            bytes_accessed=work * 2 * dof * (dof + wide),
            transcendentals=0,
        ),
        compiler_params=pltpu.CompilerParams(vmem_limit_bytes=ROOM),
    )(codes, adjoint, off)


def local_kernel(
    inst, insts, couple, first, kept, codes, here, table, left, right, adj_all, near_all, far_all,
    relay_all, arrived, state, diag, off, grad, step, base, *rest,
):
    acc = rest[-1]
    row = pl.program_id(0)
    blocks = pl.num_programs(0)

    @pl.when(row == 0)
    def _():
        acc[...] = jnp.zeros_like(acc)

    acc[row] += transposed_product(diag[0, 0], state[0, 0])
    for slot in range(couple):
        code = codes[slot, row]

        @pl.when(code < blocks)
        def _():
            term = transposed_product(off[0, 0, slot], state[0, 0]).astype(jnp.bfloat16)
            acc[code] += term.astype(jnp.float32)

    @pl.when(row == blocks - 1)
    def _():
        odd = parity()
        for slot in range(arrived.shape[1]):
            block = jnp.where(odd == 0, left[0, slot], right[0, slot])
            acc[block] += arrived[0, slot].astype(jnp.float32)

        def mix(total, block, sources, at):
            for index, source in enumerate(sources):
                for other in range(insts):
                    sender = here[0] ^ (at + index)
                    weight = table[sender * insts + other, here[0] * insts + inst]
                    total += weight * source[other, block].astype(jnp.float32)
            return total

        def finish(block, carry):
            total = acc[block] - grad[0, block].astype(jnp.float32)
            total = mix(total, block, (adj_all, near_all), 0)
            mine = adj_all[inst, block].astype(jnp.float32)
            base[0, block] = mine - step[0, block] * total
            if kept:
                low = base.shape[2] - kept
                rest[1][block] = jnp.broadcast_to(step[0, block, low:], rest[1].shape[1:])
            return carry

        def finish_far(block, carry):
            total = mix(jnp.zeros(acc.shape[1:], jnp.float32), block, (far_all, relay_all), 2)
            base[0, block] -= step[0, block] * total
            return carry

        lax.fori_loop(0, base.shape[1], finish, 0)
        lax.fori_loop(0, first, finish_far, 0)
        if kept:
            rest[0][...] = base[:, :, base.shape[2] - kept :]


def local_part(
    inst, kept, codes, here, table, left, right, adjoint, near, far, relay, arrived, diag, off, grad, step
):
    insts, blocks, dof, wide = adjoint.shape
    couple = off.shape[2]
    first = far.shape[1]

    once = functools.partial(pl.BlockSpec, pipeline_mode=pl.Buffered(1))
    whole = lambda x: once(x.shape, lambda r: (0, 0, 0, 0))

    shapes = [jax.ShapeDtypeStruct((1, blocks, dof, wide), jnp.float32)]
    if kept:
        shapes.append(pltpu.VMEM((1, blocks, kept, wide), jnp.float32))
        shapes.append(pltpu.VMEM((blocks, kept, 128), jnp.float32))
    return pl.pallas_call(
        functools.partial(local_kernel, inst, insts, couple, first, kept),
        grid=(blocks,),
        out_shape=shapes,
        in_specs=[
            SMEM,
            SMEM,
            SMEM,
            SMEM,
            SMEM,
            whole(adjoint),
            whole(near),
            whole(far),
            whole(relay),
            whole(arrived),
            pl.BlockSpec((1, 1, dof, wide), lambda r: (inst, r, 0, 0)),
            pl.BlockSpec((1, 1, dof, dof), lambda r: (inst, r, 0, 0)),
            pl.BlockSpec((1, 1, couple, dof, dof), lambda r: (inst, r, 0, 0, 0)),
            once((1, blocks, dof, wide), lambda r: (inst, 0, 0, 0)),
            once((1, blocks, dof, 1), lambda r: (inst, 0, 0, 0)),
        ],
        out_specs=[
            pl.BlockSpec((1, blocks, dof, wide), lambda r: (0, 0, 0, 0)),
            *[VMEM] * (len(shapes) - 1),
        ],
        scratch_shapes=[pltpu.VMEM((blocks, dof, wide), jnp.float32)],
        compiler_params=pltpu.CompilerParams(vmem_limit_bytes=LOCAL_ROOM),
        cost_estimate=pl.CostEstimate(
            flops=4 * blocks * dof * dof * wide,
            bytes_accessed=blocks * dof * (6 * dof + 12 * wide),
            transcendentals=0,
        ),
    )(
        codes, here, table, left, right, adjoint, near, far, relay, arrived, adjoint, diag, off,
        grad, step,
    )


def mix_kernel(insts, pieces, here, table, own, near, *outs):
    for inst in range(insts):
        total = None
        for index, source in enumerate((own, near)):
            for other in range(insts):
                sender, target = here[0] ^ index, here[0] ^ 2
                weight = table[sender * insts + other, target * insts + inst]
                term = weight * source[other, 0].astype(jnp.float32)
                total = term if total is None else total + term
        total = total.astype(jnp.bfloat16)
        for out, (which, low, high) in zip(outs, pieces):
            if which == inst:
                out[0, 0] = total[low:high]


def mix(here, table, adjoint, near, first, pieces):
    insts, blocks, dof, wide = adjoint.shape
    state = pl.BlockSpec((insts, 1, dof, wide), lambda r: (0, r + first, 0, 0))
    count = blocks - first
    return pl.pallas_call(
        functools.partial(mix_kernel, insts, pieces),
        grid=(count,),
        out_shape=[
            jax.ShapeDtypeStruct((1, count, high - low, wide), jnp.bfloat16)
            for _, low, high in pieces
        ],
        in_specs=[SMEM, SMEM, state, state],
        out_specs=[
            pl.BlockSpec((1, 1, high - low, wide), lambda r: (0, r, 0, 0))
            for _, low, high in pieces
        ],
        cost_estimate=pl.CostEstimate(
            flops=8 * insts * count * dof * wide,
            bytes_accessed=6 * insts * count * dof * wide,
            transcendentals=0,
        ),
        compiler_params=pltpu.CompilerParams(vmem_limit_bytes=ROOM),
        name="mix",
    )(here, table, adjoint, near)


def face_of(left, right, slot, odd):
    return jnp.where(odd == 0, right[0, slot], left[0, slot])


def final_kernel(group, first, offsets, left, right, base, step, far, *rest):
    arrivals = rest[: len(offsets)]
    out, total = rest[-2:]
    start = pl.program_id(0) * group
    odd = parity()
    slots = [(x, s, offset + s) for x, offset in zip(arrivals, offsets) for s in range(x.shape[1])]

    def one(inner, carry):
        block = start + inner
        chosen = [face_of(left, right, s, odd) == block for _, _, s in slots]
        update(
            base.at[0, inner], step[0, inner], far.at[0], slots, chosen, block, first,
            out.at[0, inner], total,
        )
        return carry

    lax.fori_loop(0, group, one, 0)


def update(base, step, far, slots, chosen, block, first, out, total):
    place = jnp.maximum(block - first, 0)
    touched = functools.reduce(jnp.logical_or, chosen)
    late = block >= first

    def put(value):
        out[...] = (base[...] - step * value).astype(jnp.bfloat16)

    @pl.when(late & ~touched)
    def _():
        put(far[place].astype(jnp.float32))

    @pl.when(~late & ~touched)
    def _():
        out[...] = base[...].astype(jnp.bfloat16)

    @pl.when(touched)
    def _():
        total[...] = jnp.where(late, far[place].astype(jnp.float32), 0.0)
        for (arrived, slot, _), hit in zip(slots, chosen):

            @pl.when(hit)
            def _():
                total[...] += arrived[0, slot].astype(jnp.float32)

        put(total[...])


def final_part(inst, row_low, row_high, group, left, right, base, step, far, arrivals, limit, out):
    insts = step.shape[0]
    _, blocks, dof, wide = base.shape
    rows = row_high - row_low
    at = row_low // rows
    first = blocks - far.shape[1]
    state = pl.BlockSpec((1, group, rows, wide), lambda g: (inst, g, at, 0))
    whole = lambda x: pl.BlockSpec(x.shape, lambda g: (0, 0, 0, 0), pipeline_mode=pl.Buffered(1))
    terms = [x for _, x in arrivals]
    operands = [left, right, base, step, far, *terms]
    specs = [
        SMEM,
        SMEM,
        pl.BlockSpec((1, group, rows, wide), lambda g: (0, g, at, 0)),
        pl.BlockSpec((1, group, rows, 1), lambda g: (inst, g, at, 0)),
        whole(far),
        *[whole(x) for x in terms],
    ]
    aliases = {}
    if out is not None:
        aliases = {len(operands): 0}
        operands.append(out)
        specs.append(ANY)
    return pl.pallas_call(
        functools.partial(final_kernel, group, first, [offset for offset, _ in arrivals]),
        grid=(blocks // group,),
        out_shape=jax.ShapeDtypeStruct((insts, blocks, dof, wide), jnp.bfloat16),
        in_specs=specs,
        out_specs=state,
        scratch_shapes=[pltpu.VMEM((rows, wide), jnp.float32)],
        input_output_aliases=aliases,
        cost_estimate=pl.CostEstimate(
            flops=20 * blocks * rows * wide,
            bytes_accessed=10 * blocks * rows * wide,
            transcendentals=0,
        ),
        compiler_params=pltpu.CompilerParams(vmem_limit_bytes=limit << 20),
    )(*operands)


def last_kernel(inst, row_low, left, right, base, step, far, arrived, old, out_hbm, total, out, sem):
    _, blocks, rows, wide = base.shape
    first = blocks - far.shape[1]
    odd = parity()
    slots = [(arrived, s, s) for s in range(arrived.shape[1])]
    faces = [face_of(left, right, s, odd) for _, _, s in slots]

    def write(block):
        target = out_hbm.at[inst, block, pl.ds(row_low, rows)]
        return pltpu.make_async_copy(out.at[block], target, sem.at[block])

    for block in range(blocks):
        chosen = [face == block for face in faces]
        spread = jnp.concatenate([step[block]] * (wide // 128), axis=-1)
        update(
            base.at[0, block], spread, far.at[0], slots, chosen, block, first,
            out.at[block], total,
        )
        write(block).start()
    for block in range(blocks):
        write(block).wait()


def last_part(inst, row_low, left, right, base, step, far, arrived, out):
    _, blocks, rows, wide = base.shape
    near_by = [pltpu.with_memory_space_constraint(x, pltpu.VMEM) for x in (far, arrived)]
    return pl.pallas_call(
        functools.partial(last_kernel, inst, row_low),
        out_shape=jax.ShapeDtypeStruct(out.shape, jnp.bfloat16),
        in_specs=[SMEM, SMEM, VMEM, VMEM, VMEM, VMEM, ANY],
        out_specs=ANY,
        scratch_shapes=[
            pltpu.VMEM((rows, wide), jnp.float32),
            pltpu.VMEM((blocks, rows, wide), jnp.bfloat16),
            pltpu.SemaphoreType.DMA((blocks,)),
        ],
        input_output_aliases={6: 0},
        cost_estimate=pl.CostEstimate(
            flops=20 * blocks * rows * wide,
            bytes_accessed=10 * blocks * rows * wide,
            transcendentals=0,
        ),
        compiler_params=pltpu.CompilerParams(vmem_limit_bytes=8 << 20),
        name="last",
    )(left, right, base, step, *near_by, out)


def per_device(adjoint, diag, off, off_columns, left, right, grad, step):
    insts, _, dof, _ = adjoint.shape
    iface = left.shape[1]
    parts, times = lax.axis_size("space"), lax.axis_size("tm")
    if times != 4 or insts != 2 or parts % 2:
        raise ValueError("unsupported mesh")
    instances = insts * times
    here = lax.axis_index("tm").astype(jnp.int32)[None]
    table = jnp.asarray(time_table(instances), dtype=jnp.float32)
    swap_core = [(i, i ^ 1) for i in range(times)]
    swap_chip = [(i, i ^ 2) for i in range(times)]
    pair = [(i, i ^ 1) for i in range(parts)]
    other = [(i, (i + 2 * (i % 2) - 1) % parts) for i in range(parts)]
    codes = off_columns.T
    cut, first, half = 256, 2, iface // 2

    ranges, pieces = [(0, half, iface - half)], [(0, iface - half, 0, dof)]
    pair0a, passed = remote_terms(0, iface, ranges, pieces, codes, adjoint, off, first)
    far0 = lax.ppermute(passed, "tm", swap_chip)
    from_pair0a = lax.ppermute(pair0a, "space", pair)
    near = lax.ppermute(adjoint, "tm", swap_core)
    ranges = [(1, 0, iface), (0, 0, half)]
    pieces = [(0, iface, 0, dof), (iface, iface + half, 0, dof)]
    other0, pair0b = remote_terms(0, iface, ranges, pieces, codes, adjoint, off)
    from_other0 = lax.ppermute(other0, "space", other)
    from_pair0b = lax.ppermute(pair0b, "space", pair)
    mixed = mix(here, table, adjoint, near, first, [(0, 0, dof), (1, 0, cut), (1, cut, dof)])
    far1 = lax.ppermute(mixed[0], "tm", swap_chip)
    far2a = lax.ppermute(mixed[1], "tm", swap_chip)
    far2b = lax.ppermute(mixed[2], "tm", swap_chip)
    ranges = [(1, 0, iface), (0, 0, iface)]
    pieces = [(0, iface, 0, dof), (iface, 2 * iface, 0, cut), (iface, 2 * iface, cut, dof)]
    other1, pair1a, pair1b = remote_terms(1, iface, ranges, pieces, codes, adjoint, off)
    from_other1 = lax.ppermute(other1, "space", other)
    from_pair1a = lax.ppermute(pair1a, "space", pair)
    from_pair1b = lax.ppermute(pair1b, "space", pair)
    relay = lax.ppermute(far0, "tm", swap_core)
    step = step[..., None]
    common = (codes, here, table, left, right, adjoint, near, far0, relay)
    (base0,) = local_part(0, 0, *common, from_other0, diag, off, grad, step)
    base1, base1b, step1b = local_part(1, dof - cut, *common, from_other1, diag, off, grad, step)
    faces = (left, right)
    arrivals = [(half, from_pair0a), (0, from_pair0b)]
    out = final_part(0, 0, dof, 2, *faces, base0, step, far1, arrivals, 58, None)
    out = final_part(1, 0, cut, 4, *faces, base1, step, far2a, [(0, from_pair1a)], 58, out)
    return last_part(1, cut, *faces, base1b, step1b, far2b, from_pair1b, out)


def solution(mesh):
    in_specs = (
        P("tm", "space", None, None),
        P("tm", "space", None, None),
        P("tm", "space", None, None, None),
        P("space", None),
        P("space", None),
        P("space", None),
        P("tm", "space", None, None),
        P("tm", "space", None),
    )
    out_specs = P("tm", "space", None, None)
    return jax.shard_map(
        per_device, mesh=mesh, in_specs=in_specs, out_specs=out_specs, check_vma=False
    )
```

```python
import functools
import math

import jax
import jax.numpy as jnp
from jax import lax
from jax.experimental import pallas as pl
from jax.experimental.pallas import tpu as pltpu
from jax.sharding import PartitionSpec as P


ANY = pl.BlockSpec(memory_space=pl.ANY)
SMEM = pl.BlockSpec(memory_space=pltpu.SMEM)
VMEM = pl.BlockSpec(memory_space=pltpu.VMEM)
SLOTS = 3
ROOM = 56 << 20
LOCAL_ROOM = 58 << 20


def time_table(count):
    table = []
    for first in range(count):
        row_values = []
        for second in range(count):
            if first != second:
                delta = first - second
                parity = 1.0 - 2.0 * (delta % 2)
                row_values.append(0.5 * parity / math.tan(math.pi * delta / count))
            else:
                row_values.append(0.0)
        table.append(row_values)
    return table


def transposed_product(jacobian, state):
    return lax.dot_general(
        jacobian, state, (((0,), (0,)), ((), ())), preferred_element_type=jnp.float32
    )


def parity():
    return lax.rem(lax.axis_index("space"), 2)


def remote_kernel(inst, iface, ranges, pieces, first, codes_hbm, state_hbm, off_hbm, *rest):
    outs, rest = rest[: len(pieces)], rest[len(pieces) :]
    if first:
        passed, *rest = rest
        *rest, read_sem = rest
    else:
        *rest, ready, out_sem = rest
    codes, code_sem, acc, states, jacobians, picked, places, state_sem, off_sem = rest
    load_codes = pltpu.make_async_copy(codes_hbm, codes, code_sem)
    load_codes.start()
    if first:
        source = state_hbm.at[:, pl.ds(0, first)]
        pltpu.make_async_copy(source, passed, read_sem).start()
    blocks = codes.shape[1]
    odd = parity()
    lows = (blocks + iface * (1 - odd), blocks + iface * odd)
    acc[...] = jnp.zeros_like(acc)
    load_codes.wait()

    found = jnp.int32(0)
    for term in range(codes.shape[0] * blocks):
        code = codes[term // blocks, term % blocks]
        hits, place, base = 0, 0, 0
        for kind, offset, count in ranges:
            at = code - (lows[kind] + offset)
            inside = (at >= 0) & (at < count)
            place = jnp.where(inside, at + base, place)
            hits = jnp.where(inside, 1, hits)
            base += count
        picked[found] = term
        places[found] = place
        found = found + hits

    def copies(index):
        slot = lax.rem(index, SLOTS)
        term = picked[index]
        row = lax.rem(term, blocks)
        return (
            pltpu.make_async_copy(state_hbm.at[inst, row], states.at[slot], state_sem.at[slot]),
            pltpu.make_async_copy(
                off_hbm.at[inst, row, lax.div(term, blocks)], jacobians.at[slot], off_sem.at[slot]
            ),
        )

    for ahead in range(SLOTS - 1):

        @pl.when(ahead < found)
        def _():
            for copy in copies(jnp.int32(ahead)):
                copy.start()

    def one(index, carry):
        @pl.when(index + SLOTS - 1 < found)
        def _():
            for copy in copies(index + SLOTS - 1):
                copy.start()

        for copy in copies(index):
            copy.wait()
        slot = lax.rem(index, SLOTS)
        term = transposed_product(jacobians[slot], states[slot]).astype(jnp.bfloat16)
        acc[places[index]] += term.astype(jnp.float32)
        return carry

    lax.fori_loop(0, found, one, 0)
    if first:
        for out, (slot_low, slot_high, row_low, row_high) in zip(outs, pieces):
            for slot in range(slot_low, slot_high):
                out[0, slot - slot_low] = acc[slot, row_low:row_high].astype(jnp.bfloat16)
        pltpu.make_async_copy(source, passed, read_sem).wait()
        return
    writes = []
    for slot in range(acc.shape[0]):
        ready[slot] = acc[slot].astype(jnp.bfloat16)
        for out, (slot_low, slot_high, row_low, row_high) in zip(outs, pieces):
            if slot_low <= slot < slot_high:
                piece = ready.at[slot, pl.ds(row_low, row_high - row_low)]
                copy = pltpu.make_async_copy(
                    piece, out.at[0, slot - slot_low], out_sem.at[len(writes)]
                )
                copy.start()
                writes.append(copy)
    for copy in writes:
        copy.wait()


def remote_terms(inst, iface, ranges, pieces, codes, adjoint, off, first=0):
    insts, blocks, dof, wide = adjoint.shape
    couple = off.shape[2]
    work = sum(count for _, _, count in ranges)
    shapes = [(1, b - a, d - c, wide) for a, b, c, d in pieces]
    if first:
        shapes.append((insts, first, dof, wide))
        shapes = [pltpu.VMEM(shape, jnp.bfloat16) for shape in shapes]
        out_specs = [VMEM] * len(shapes)
        extra = [pltpu.SemaphoreType.DMA(())]
    else:
        shapes = [jax.ShapeDtypeStruct(shape, jnp.bfloat16) for shape in shapes]
        out_specs = [ANY] * len(shapes)
        extra = [
            pltpu.VMEM((work, dof, wide), jnp.bfloat16),
            pltpu.SemaphoreType.DMA((sum(b - a for a, b, _, _ in pieces),)),
        ]
    return pl.pallas_call(
        functools.partial(remote_kernel, inst, iface, ranges, pieces, first),
        out_shape=shapes,
        in_specs=[ANY, ANY, ANY],
        out_specs=out_specs,
        scratch_shapes=[
            pltpu.SMEM((couple, blocks), jnp.int32),
            pltpu.SemaphoreType.DMA(()),
            pltpu.VMEM((work, dof, wide), jnp.float32),
            pltpu.VMEM((SLOTS, dof, wide), jnp.bfloat16),
            pltpu.VMEM((SLOTS, dof, dof), jnp.bfloat16),
            pltpu.SMEM((couple * blocks + 1,), jnp.int32),
            pltpu.SMEM((couple * blocks + 1,), jnp.int32),
            pltpu.SemaphoreType.DMA((SLOTS,)),
            pltpu.SemaphoreType.DMA((SLOTS,)),
            *extra,
        ],
        cost_estimate=pl.CostEstimate(
            flops=2 * work * dof * dof * wide,
            bytes_accessed=work * 2 * dof * (dof + wide),
            transcendentals=0,
        ),
        compiler_params=pltpu.CompilerParams(vmem_limit_bytes=ROOM),
    )(codes, adjoint, off)


def local_kernel(
    inst, insts, couple, first, kept, codes, here, table, left, right, adj_all, near_all, far_all,
    relay_all, arrived, state, diag, off, grad, step, base, *rest,
):
    acc = rest[-1]
    row = pl.program_id(0)
    blocks = pl.num_programs(0)

    @pl.when(row == 0)
    def _():
        acc[...] = jnp.zeros_like(acc)

    acc[row] += transposed_product(diag[0, 0], state[0, 0])
    for slot in range(couple):
        code = codes[slot, row]

        @pl.when(code < blocks)
        def _():
            term = transposed_product(off[0, 0, slot], state[0, 0]).astype(jnp.bfloat16)
            acc[code] += term.astype(jnp.float32)

    @pl.when(row == blocks - 1)
    def _():
        odd = parity()
        for slot in range(arrived.shape[1]):
            block = jnp.where(odd == 0, left[0, slot], right[0, slot])
            acc[block] += arrived[0, slot].astype(jnp.float32)

        def mix(total, block, sources, at):
            for index, source in enumerate(sources):
                for other in range(insts):
                    sender = here[0] ^ (at + index)
                    weight = table[sender * insts + other, here[0] * insts + inst]
                    total += weight * source[other, block].astype(jnp.float32)
            return total

        def finish(block, carry):
            total = acc[block] - grad[0, block].astype(jnp.float32)
            total = mix(total, block, (adj_all, near_all), 0)
            mine = adj_all[inst, block].astype(jnp.float32)
            base[0, block] = mine - step[0, block] * total
            if kept:
                low = base.shape[2] - kept
                rest[1][block] = jnp.broadcast_to(step[0, block, low:], rest[1].shape[1:])
            return carry

        def finish_far(block, carry):
            total = mix(jnp.zeros(acc.shape[1:], jnp.float32), block, (far_all, relay_all), 2)
            base[0, block] -= step[0, block] * total
            return carry

        lax.fori_loop(0, base.shape[1], finish, 0)
        lax.fori_loop(0, first, finish_far, 0)
        if kept:
            rest[0][...] = base[:, :, base.shape[2] - kept :]


def local_part(
    inst, kept, codes, here, table, left, right, adjoint, near, far, relay, arrived, diag, off, grad, step
):
    insts, blocks, dof, wide = adjoint.shape
    couple = off.shape[2]
    first = far.shape[1]

    once = functools.partial(pl.BlockSpec, pipeline_mode=pl.Buffered(1))
    whole = lambda x: once(x.shape, lambda r: (0, 0, 0, 0))

    shapes = [jax.ShapeDtypeStruct((1, blocks, dof, wide), jnp.float32)]
    if kept:
        shapes.append(pltpu.VMEM((1, blocks, kept, wide), jnp.float32))
        shapes.append(pltpu.VMEM((blocks, kept, 128), jnp.float32))
    return pl.pallas_call(
        functools.partial(local_kernel, inst, insts, couple, first, kept),
        grid=(blocks,),
        out_shape=shapes,
        in_specs=[
            SMEM,
            SMEM,
            SMEM,
            SMEM,
            SMEM,
            whole(adjoint),
            whole(near),
            whole(far),
            whole(relay),
            whole(arrived),
            pl.BlockSpec((1, 1, dof, wide), lambda r: (inst, r, 0, 0)),
            pl.BlockSpec((1, 1, dof, dof), lambda r: (inst, r, 0, 0)),
            pl.BlockSpec((1, 1, couple, dof, dof), lambda r: (inst, r, 0, 0, 0)),
            once((1, blocks, dof, wide), lambda r: (inst, 0, 0, 0)),
            once((1, blocks, dof, 1), lambda r: (inst, 0, 0, 0)),
        ],
        out_specs=[
            pl.BlockSpec((1, blocks, dof, wide), lambda r: (0, 0, 0, 0)),
            *[VMEM] * (len(shapes) - 1),
        ],
        scratch_shapes=[pltpu.VMEM((blocks, dof, wide), jnp.float32)],
        compiler_params=pltpu.CompilerParams(vmem_limit_bytes=LOCAL_ROOM),
        cost_estimate=pl.CostEstimate(
            flops=4 * blocks * dof * dof * wide,
            bytes_accessed=blocks * dof * (6 * dof + 12 * wide),
            transcendentals=0,
        ),
    )(
        codes, here, table, left, right, adjoint, near, far, relay, arrived, adjoint, diag, off,
        grad, step,
    )


def mix_kernel(insts, pieces, here, table, own, near, *outs):
    for inst in range(insts):
        total = None
        for index, source in enumerate((own, near)):
            for other in range(insts):
                sender, target = here[0] ^ index, here[0] ^ 2
                weight = table[sender * insts + other, target * insts + inst]
                term = weight * source[other, 0].astype(jnp.float32)
                total = term if total is None else total + term
        total = total.astype(jnp.bfloat16)
        for out, (which, low, high) in zip(outs, pieces):
            if which == inst:
                out[0, 0] = total[low:high]


def mix(here, table, adjoint, near, first, pieces):
    insts, blocks, dof, wide = adjoint.shape
    state = pl.BlockSpec((insts, 1, dof, wide), lambda r: (0, r + first, 0, 0))
    count = blocks - first
    return pl.pallas_call(
        functools.partial(mix_kernel, insts, pieces),
        grid=(count,),
        out_shape=[
            jax.ShapeDtypeStruct((1, count, high - low, wide), jnp.bfloat16)
            for _, low, high in pieces
        ],
        in_specs=[SMEM, SMEM, state, state],
        out_specs=[
            pl.BlockSpec((1, 1, high - low, wide), lambda r: (0, r, 0, 0))
            for _, low, high in pieces
        ],
        cost_estimate=pl.CostEstimate(
            flops=8 * insts * count * dof * wide,
            bytes_accessed=6 * insts * count * dof * wide,
            transcendentals=0,
        ),
        compiler_params=pltpu.CompilerParams(vmem_limit_bytes=ROOM),
        name="mix",
    )(here, table, adjoint, near)


def face_of(left, right, slot, odd):
    return jnp.where(odd == 0, right[0, slot], left[0, slot])


def final_kernel(group, first, offsets, left, right, base, step, far, *rest):
    arrivals = rest[: len(offsets)]
    out, total = rest[-2:]
    start = pl.program_id(0) * group
    odd = parity()
    slots = [(x, s, offset + s) for x, offset in zip(arrivals, offsets) for s in range(x.shape[1])]

    def one(inner, carry):
        block = start + inner
        chosen = [face_of(left, right, s, odd) == block for _, _, s in slots]
        update(
            base.at[0, inner], step[0, inner], far.at[0], slots, chosen, block, first,
            out.at[0, inner], total,
        )
        return carry

    lax.fori_loop(0, group, one, 0)


def update(base, step, far, slots, chosen, block, first, out, total):
    place = jnp.maximum(block - first, 0)
    touched = functools.reduce(jnp.logical_or, chosen)
    late = block >= first

    def put(value):
        out[...] = (base[...] - step * value).astype(jnp.bfloat16)

    @pl.when(late & ~touched)
    def _():
        put(far[place].astype(jnp.float32))

    @pl.when(~late & ~touched)
    def _():
        out[...] = base[...].astype(jnp.bfloat16)

    @pl.when(touched)
    def _():
        total[...] = jnp.where(late, far[place].astype(jnp.float32), 0.0)
        for (arrived, slot, _), hit in zip(slots, chosen):

            @pl.when(hit)
            def _():
                total[...] += arrived[0, slot].astype(jnp.float32)

        put(total[...])


def final_part(inst, row_low, row_high, group, left, right, base, step, far, arrivals, limit, out):
    insts = step.shape[0]
    _, blocks, dof, wide = base.shape
    rows = row_high - row_low
    at = row_low // rows
    first = blocks - far.shape[1]
    state = pl.BlockSpec((1, group, rows, wide), lambda g: (inst, g, at, 0))
    whole = lambda x: pl.BlockSpec(x.shape, lambda g: (0, 0, 0, 0), pipeline_mode=pl.Buffered(1))
    terms = [x for _, x in arrivals]
    operands = [left, right, base, step, far, *terms]
    specs = [
        SMEM,
        SMEM,
        pl.BlockSpec((1, group, rows, wide), lambda g: (0, g, at, 0)),
        pl.BlockSpec((1, group, rows, 1), lambda g: (inst, g, at, 0)),
        whole(far),
        *[whole(x) for x in terms],
    ]
    aliases = {}
    if out is not None:
        aliases = {len(operands): 0}
        operands.append(out)
        specs.append(ANY)
    return pl.pallas_call(
        functools.partial(final_kernel, group, first, [offset for offset, _ in arrivals]),
        grid=(blocks // group,),
        out_shape=jax.ShapeDtypeStruct((insts, blocks, dof, wide), jnp.bfloat16),
        in_specs=specs,
        out_specs=state,
        scratch_shapes=[pltpu.VMEM((rows, wide), jnp.float32)],
        input_output_aliases=aliases,
        cost_estimate=pl.CostEstimate(
            flops=20 * blocks * rows * wide,
            bytes_accessed=10 * blocks * rows * wide,
            transcendentals=0,
        ),
        compiler_params=pltpu.CompilerParams(vmem_limit_bytes=limit << 20),
    )(*operands)


def last_kernel(inst, row_low, left, right, base, step, far, arrived, old, out_hbm, total, out, sem):
    _, blocks, rows, wide = base.shape
    first = blocks - far.shape[1]
    odd = parity()
    slots = [(arrived, s, s) for s in range(arrived.shape[1])]
    faces = [face_of(left, right, s, odd) for _, _, s in slots]

    def write(block):
        target = out_hbm.at[inst, block, pl.ds(row_low, rows)]
        return pltpu.make_async_copy(out.at[block], target, sem.at[block])

    for block in range(blocks):
        chosen = [face == block for face in faces]
        spread = jnp.concatenate([step[block]] * (wide // 128), axis=-1)
        update(
            base.at[0, block], spread, far.at[0], slots, chosen, block, first,
            out.at[block], total,
        )
        write(block).start()
    for block in range(blocks):
        write(block).wait()


def last_part(inst, row_low, left, right, base, step, far, arrived, out):
    _, blocks, rows, wide = base.shape
    near_by = [pltpu.with_memory_space_constraint(x, pltpu.VMEM) for x in (far, arrived)]
    return pl.pallas_call(
        functools.partial(last_kernel, inst, row_low),
        out_shape=jax.ShapeDtypeStruct(out.shape, jnp.bfloat16),
        in_specs=[SMEM, SMEM, VMEM, VMEM, VMEM, VMEM, ANY],
        out_specs=ANY,
        scratch_shapes=[
            pltpu.VMEM((rows, wide), jnp.float32),
            pltpu.VMEM((blocks, rows, wide), jnp.bfloat16),
            pltpu.SemaphoreType.DMA((blocks,)),
        ],
        input_output_aliases={6: 0},
        cost_estimate=pl.CostEstimate(
            flops=20 * blocks * rows * wide,
            bytes_accessed=10 * blocks * rows * wide,
            transcendentals=0,
        ),
        compiler_params=pltpu.CompilerParams(vmem_limit_bytes=8 << 20),
        name="last",
    )(left, right, base, step, *near_by, out)


def per_device(adjoint, diag, off, off_columns, left, right, grad, step):
    insts, _, dof, _ = adjoint.shape
    iface = left.shape[1]
    parts, times = lax.axis_size("space"), lax.axis_size("tm")
    if times != 4 or insts != 2 or parts % 2:
        raise ValueError("unsupported mesh")
    instances = insts * times
    here = lax.axis_index("tm").astype(jnp.int32)[None]
    table = jnp.asarray(time_table(instances), dtype=jnp.float32)
    swap_core = [(i, i ^ 1) for i in range(times)]
    swap_chip = [(i, i ^ 2) for i in range(times)]
    pair = [(i, i ^ 1) for i in range(parts)]
    other = [(i, (i + 2 * (i % 2) - 1) % parts) for i in range(parts)]
    codes = off_columns.T
    cut, first, half = 240, 2, iface - 1

    ranges, pieces = [(0, half, iface - half)], [(0, iface - half, 0, dof)]
    pair0a, passed = remote_terms(0, iface, ranges, pieces, codes, adjoint, off, first)
    far0 = lax.ppermute(passed, "tm", swap_chip)
    from_pair0a = lax.ppermute(pair0a, "space", pair)
    near = lax.ppermute(adjoint, "tm", swap_core)
    ranges, pieces = [(0, 0, half)], [(0, half, 0, dof)]
    (pair0b,) = remote_terms(0, iface, ranges, pieces, codes, adjoint, off)
    from_pair0b = lax.ppermute(pair0b, "space", pair)
    ranges, pieces = [(1, 0, iface)], [(0, iface, 0, dof)]
    (other0,) = remote_terms(0, iface, ranges, pieces, codes, adjoint, off)
    from_other0 = lax.ppermute(other0, "space", other)
    mixed = mix(here, table, adjoint, near, first, [(0, 0, dof), (1, 0, cut), (1, cut, dof)])
    far1 = lax.ppermute(mixed[0], "tm", swap_chip)
    far2a = lax.ppermute(mixed[1], "tm", swap_chip)
    far2b = lax.ppermute(mixed[2], "tm", swap_chip)
    ranges = [(1, 0, iface), (0, 0, iface)]
    pieces = [(0, iface, 0, dof), (iface, 2 * iface, 0, cut), (iface, 2 * iface, cut, dof)]
    other1, pair1a, pair1b = remote_terms(1, iface, ranges, pieces, codes, adjoint, off)
    from_other1 = lax.ppermute(other1, "space", other)
    from_pair1a = lax.ppermute(pair1a, "space", pair)
    from_pair1b = lax.ppermute(pair1b, "space", pair)
    relay = lax.ppermute(far0, "tm", swap_core)
    step = step[..., None]
    common = (codes, here, table, left, right, adjoint, near, far0, relay)
    (base0,) = local_part(0, 0, *common, from_other0, diag, off, grad, step)
    base1, base1b, step1b = local_part(1, dof - cut, *common, from_other1, diag, off, grad, step)
    faces = (left, right)
    arrivals = [(half, from_pair0a), (0, from_pair0b)]
    out = final_part(0, 0, dof, 2, *faces, base0, step, far1, arrivals, 58, None)
    out = final_part(1, 0, cut, 4, *faces, base1, step, far2a, [(0, from_pair1a)], 58, out)
    return last_part(1, cut, *faces, base1b, step1b, far2b, from_pair1b, out)


def solution(mesh):
    in_specs = (
        P("tm", "space", None, None),
        P("tm", "space", None, None),
        P("tm", "space", None, None, None),
        P("space", None),
        P("space", None),
        P("space", None),
        P("tm", "space", None, None),
        P("tm", "space", None),
    )
    out_specs = P("tm", "space", None, None)
    return jax.shard_map(
        per_device, mesh=mesh, in_specs=in_specs, out_specs=out_specs, check_vma=False
    )
```

```python
import functools
import math

import jax
import jax.numpy as jnp
from jax import lax
from jax.experimental import pallas as pl
from jax.experimental.pallas import tpu as pltpu
from jax.sharding import PartitionSpec as P


ANY = pl.BlockSpec(memory_space=pl.ANY)
SMEM = pl.BlockSpec(memory_space=pltpu.SMEM)
VMEM = pl.BlockSpec(memory_space=pltpu.VMEM)
SLOTS = 3
ROOM = 56 << 20
LOCAL_ROOM = 58 << 20


def time_table(count):
    table = []
    for first in range(count):
        row_values = []
        for second in range(count):
            if first != second:
                delta = first - second
                parity = 1.0 - 2.0 * (delta % 2)
                row_values.append(0.5 * parity / math.tan(math.pi * delta / count))
            else:
                row_values.append(0.0)
        table.append(row_values)
    return table


def transposed_product(jacobian, state):
    return lax.dot_general(
        jacobian, state, (((0,), (0,)), ((), ())), preferred_element_type=jnp.float32
    )


def parity():
    return lax.rem(lax.axis_index("space"), 2)


def remote_kernel(inst, iface, ranges, pieces, first, codes_hbm, state_hbm, off_hbm, *rest):
    outs, rest = rest[: len(pieces)], rest[len(pieces) :]
    if first:
        passed, *rest = rest
        *rest, read_sem = rest
    else:
        *rest, ready, out_sem = rest
    codes, code_sem, acc, states, jacobians, picked, places, state_sem, off_sem = rest
    load_codes = pltpu.make_async_copy(codes_hbm, codes, code_sem)
    load_codes.start()
    if first:
        source = state_hbm.at[:, pl.ds(0, first)]
        pltpu.make_async_copy(source, passed, read_sem).start()
    blocks = codes.shape[1]
    odd = parity()
    lows = (blocks + iface * (1 - odd), blocks + iface * odd)
    acc[...] = jnp.zeros_like(acc)
    load_codes.wait()

    found = jnp.int32(0)
    for term in range(codes.shape[0] * blocks):
        code = codes[term // blocks, term % blocks]
        hits, place, base = 0, 0, 0
        for kind, offset, count in ranges:
            at = code - (lows[kind] + offset)
            inside = (at >= 0) & (at < count)
            place = jnp.where(inside, at + base, place)
            hits = jnp.where(inside, 1, hits)
            base += count
        picked[found] = term
        places[found] = place
        found = found + hits

    def copies(index):
        slot = lax.rem(index, SLOTS)
        term = picked[index]
        row = lax.rem(term, blocks)
        return (
            pltpu.make_async_copy(state_hbm.at[inst, row], states.at[slot], state_sem.at[slot]),
            pltpu.make_async_copy(
                off_hbm.at[inst, row, lax.div(term, blocks)], jacobians.at[slot], off_sem.at[slot]
            ),
        )

    for ahead in range(SLOTS - 1):

        @pl.when(ahead < found)
        def _():
            for copy in copies(jnp.int32(ahead)):
                copy.start()

    def one(index, carry):
        @pl.when(index + SLOTS - 1 < found)
        def _():
            for copy in copies(index + SLOTS - 1):
                copy.start()

        for copy in copies(index):
            copy.wait()
        slot = lax.rem(index, SLOTS)
        term = transposed_product(jacobians[slot], states[slot]).astype(jnp.bfloat16)
        acc[places[index]] += term.astype(jnp.float32)
        return carry

    lax.fori_loop(0, found, one, 0)
    if first:
        for out, (slot_low, slot_high, row_low, row_high) in zip(outs, pieces):
            for slot in range(slot_low, slot_high):
                out[0, slot - slot_low] = acc[slot, row_low:row_high].astype(jnp.bfloat16)
        pltpu.make_async_copy(source, passed, read_sem).wait()
        return
    writes = []
    for slot in range(acc.shape[0]):
        ready[slot] = acc[slot].astype(jnp.bfloat16)
        for out, (slot_low, slot_high, row_low, row_high) in zip(outs, pieces):
            if slot_low <= slot < slot_high:
                piece = ready.at[slot, pl.ds(row_low, row_high - row_low)]
                copy = pltpu.make_async_copy(
                    piece, out.at[0, slot - slot_low], out_sem.at[len(writes)]
                )
                copy.start()
                writes.append(copy)
    for copy in writes:
        copy.wait()


def remote_terms(inst, iface, ranges, pieces, codes, adjoint, off, first=0):
    insts, blocks, dof, wide = adjoint.shape
    couple = off.shape[2]
    work = sum(count for _, _, count in ranges)
    shapes = [(1, b - a, d - c, wide) for a, b, c, d in pieces]
    if first:
        shapes.append((insts, first, dof, wide))
        shapes = [pltpu.VMEM(shape, jnp.bfloat16) for shape in shapes]
        out_specs = [VMEM] * len(shapes)
        extra = [pltpu.SemaphoreType.DMA(())]
    else:
        shapes = [jax.ShapeDtypeStruct(shape, jnp.bfloat16) for shape in shapes]
        out_specs = [ANY] * len(shapes)
        extra = [
            pltpu.VMEM((work, dof, wide), jnp.bfloat16),
            pltpu.SemaphoreType.DMA((sum(b - a for a, b, _, _ in pieces),)),
        ]
    return pl.pallas_call(
        functools.partial(remote_kernel, inst, iface, ranges, pieces, first),
        out_shape=shapes,
        in_specs=[ANY, ANY, ANY],
        out_specs=out_specs,
        scratch_shapes=[
            pltpu.SMEM((couple, blocks), jnp.int32),
            pltpu.SemaphoreType.DMA(()),
            pltpu.VMEM((work, dof, wide), jnp.float32),
            pltpu.VMEM((SLOTS, dof, wide), jnp.bfloat16),
            pltpu.VMEM((SLOTS, dof, dof), jnp.bfloat16),
            pltpu.SMEM((couple * blocks + 1,), jnp.int32),
            pltpu.SMEM((couple * blocks + 1,), jnp.int32),
            pltpu.SemaphoreType.DMA((SLOTS,)),
            pltpu.SemaphoreType.DMA((SLOTS,)),
            *extra,
        ],
        cost_estimate=pl.CostEstimate(
            flops=2 * work * dof * dof * wide,
            bytes_accessed=work * 2 * dof * (dof + wide),
            transcendentals=0,
        ),
        compiler_params=pltpu.CompilerParams(vmem_limit_bytes=ROOM),
    )(codes, adjoint, off)


def local_kernel(
    inst, insts, couple, first, kept, codes, here, table, left, right, adj_all, near_all, far_all,
    relay_all, arrived, state, diag, off, grad, step, base, *rest,
):
    acc = rest[-1]
    row = pl.program_id(0)
    blocks = pl.num_programs(0)

    @pl.when(row == 0)
    def _():
        acc[...] = jnp.zeros_like(acc)

    acc[row] += transposed_product(diag[0, 0], state[0, 0])
    for slot in range(couple):
        code = codes[slot, row]

        @pl.when(code < blocks)
        def _():
            term = transposed_product(off[0, 0, slot], state[0, 0]).astype(jnp.bfloat16)
            acc[code] += term.astype(jnp.float32)

    @pl.when(row == blocks - 1)
    def _():
        odd = parity()
        for slot in range(arrived.shape[1]):
            block = jnp.where(odd == 0, left[0, slot], right[0, slot])
            acc[block] += arrived[0, slot].astype(jnp.float32)

        def mix(total, block, sources, at):
            for index, source in enumerate(sources):
                for other in range(insts):
                    sender = here[0] ^ (at + index)
                    weight = table[sender * insts + other, here[0] * insts + inst]
                    total += weight * source[other, block].astype(jnp.float32)
            return total

        def finish(block, carry):
            total = acc[block] - grad[0, block].astype(jnp.float32)
            total = mix(total, block, (adj_all, near_all), 0)
            mine = adj_all[inst, block].astype(jnp.float32)
            base[0, block] = mine - step[0, block] * total
            if kept:
                low = base.shape[2] - kept
                rest[1][block] = jnp.broadcast_to(step[0, block, low:], rest[1].shape[1:])
            return carry

        def finish_far(block, carry):
            total = mix(jnp.zeros(acc.shape[1:], jnp.float32), block, (far_all, relay_all), 2)
            base[0, block] -= step[0, block] * total
            return carry

        lax.fori_loop(0, base.shape[1], finish, 0)
        lax.fori_loop(0, first, finish_far, 0)
        if kept:
            rest[0][...] = base[:, :, base.shape[2] - kept :]


def local_part(
    inst, kept, codes, here, table, left, right, adjoint, near, far, relay, arrived, diag, off, grad, step
):
    insts, blocks, dof, wide = adjoint.shape
    couple = off.shape[2]
    first = far.shape[1]

    once = functools.partial(pl.BlockSpec, pipeline_mode=pl.Buffered(1))
    whole = lambda x: once(x.shape, lambda r: (0, 0, 0, 0))

    shapes = [jax.ShapeDtypeStruct((1, blocks, dof, wide), jnp.float32)]
    if kept:
        shapes.append(pltpu.VMEM((1, blocks, kept, wide), jnp.float32))
        shapes.append(pltpu.VMEM((blocks, kept, 128), jnp.float32))
    return pl.pallas_call(
        functools.partial(local_kernel, inst, insts, couple, first, kept),
        grid=(blocks,),
        out_shape=shapes,
        in_specs=[
            SMEM,
            SMEM,
            SMEM,
            SMEM,
            SMEM,
            whole(adjoint),
            whole(near),
            whole(far),
            whole(relay),
            whole(arrived),
            pl.BlockSpec((1, 1, dof, wide), lambda r: (inst, r, 0, 0)),
            pl.BlockSpec((1, 1, dof, dof), lambda r: (inst, r, 0, 0)),
            pl.BlockSpec((1, 1, couple, dof, dof), lambda r: (inst, r, 0, 0, 0)),
            once((1, blocks, dof, wide), lambda r: (inst, 0, 0, 0)),
            once((1, blocks, dof, 1), lambda r: (inst, 0, 0, 0)),
        ],
        out_specs=[
            pl.BlockSpec((1, blocks, dof, wide), lambda r: (0, 0, 0, 0)),
            *[VMEM] * (len(shapes) - 1),
        ],
        scratch_shapes=[pltpu.VMEM((blocks, dof, wide), jnp.float32)],
        compiler_params=pltpu.CompilerParams(vmem_limit_bytes=LOCAL_ROOM),
        cost_estimate=pl.CostEstimate(
            flops=4 * blocks * dof * dof * wide,
            bytes_accessed=blocks * dof * (6 * dof + 12 * wide),
            transcendentals=0,
        ),
    )(
        codes, here, table, left, right, adjoint, near, far, relay, arrived, adjoint, diag, off,
        grad, step,
    )


def mix_kernel(insts, pieces, here, table, own, near, *outs):
    for inst in range(insts):
        total = None
        for index, source in enumerate((own, near)):
            for other in range(insts):
                sender, target = here[0] ^ index, here[0] ^ 2
                weight = table[sender * insts + other, target * insts + inst]
                term = weight * source[other, 0].astype(jnp.float32)
                total = term if total is None else total + term
        total = total.astype(jnp.bfloat16)
        for out, (which, low, high) in zip(outs, pieces):
            if which == inst:
                out[0, 0] = total[low:high]


def mix(here, table, adjoint, near, first, pieces):
    insts, blocks, dof, wide = adjoint.shape
    state = pl.BlockSpec((insts, 1, dof, wide), lambda r: (0, r + first, 0, 0))
    count = blocks - first
    return pl.pallas_call(
        functools.partial(mix_kernel, insts, pieces),
        grid=(count,),
        out_shape=[
            jax.ShapeDtypeStruct((1, count, high - low, wide), jnp.bfloat16)
            for _, low, high in pieces
        ],
        in_specs=[SMEM, SMEM, state, state],
        out_specs=[
            pl.BlockSpec((1, 1, high - low, wide), lambda r: (0, r, 0, 0))
            for _, low, high in pieces
        ],
        cost_estimate=pl.CostEstimate(
            flops=8 * insts * count * dof * wide,
            bytes_accessed=6 * insts * count * dof * wide,
            transcendentals=0,
        ),
        compiler_params=pltpu.CompilerParams(vmem_limit_bytes=ROOM),
        name="mix",
    )(here, table, adjoint, near)


def face_of(left, right, slot, odd):
    return jnp.where(odd == 0, right[0, slot], left[0, slot])


def final_kernel(group, first, offsets, left, right, base, step, far, *rest):
    arrivals = rest[: len(offsets)]
    out, total = rest[-2:]
    start = pl.program_id(0) * group
    odd = parity()
    slots = [(x, s, offset + s) for x, offset in zip(arrivals, offsets) for s in range(x.shape[1])]

    def one(inner, carry):
        block = start + inner
        chosen = [face_of(left, right, s, odd) == block for _, _, s in slots]
        update(
            base.at[0, inner], step[0, inner], far.at[0], slots, chosen, block, first,
            out.at[0, inner], total,
        )
        return carry

    lax.fori_loop(0, group, one, 0)


def update(base, step, far, slots, chosen, block, first, out, total):
    place = jnp.maximum(block - first, 0)
    touched = functools.reduce(jnp.logical_or, chosen)
    late = block >= first

    def put(value):
        out[...] = (base[...] - step * value).astype(jnp.bfloat16)

    @pl.when(late & ~touched)
    def _():
        put(far[place].astype(jnp.float32))

    @pl.when(~late & ~touched)
    def _():
        out[...] = base[...].astype(jnp.bfloat16)

    @pl.when(touched)
    def _():
        total[...] = jnp.where(late, far[place].astype(jnp.float32), 0.0)
        for (arrived, slot, _), hit in zip(slots, chosen):

            @pl.when(hit)
            def _():
                total[...] += arrived[0, slot].astype(jnp.float32)

        put(total[...])


def final_part(inst, row_low, row_high, group, left, right, base, step, far, arrivals, limit, out):
    insts = step.shape[0]
    _, blocks, dof, wide = base.shape
    rows = row_high - row_low
    at = row_low // rows
    first = blocks - far.shape[1]
    state = pl.BlockSpec((1, group, rows, wide), lambda g: (inst, g, at, 0))
    whole = lambda x: pl.BlockSpec(x.shape, lambda g: (0, 0, 0, 0), pipeline_mode=pl.Buffered(1))
    terms = [x for _, x in arrivals]
    operands = [left, right, base, step, far, *terms]
    specs = [
        SMEM,
        SMEM,
        pl.BlockSpec((1, group, rows, wide), lambda g: (0, g, at, 0)),
        pl.BlockSpec((1, group, rows, 1), lambda g: (inst, g, at, 0)),
        whole(far),
        *[whole(x) for x in terms],
    ]
    aliases = {}
    if out is not None:
        aliases = {len(operands): 0}
        operands.append(out)
        specs.append(ANY)
    return pl.pallas_call(
        functools.partial(final_kernel, group, first, [offset for offset, _ in arrivals]),
        grid=(blocks // group,),
        out_shape=jax.ShapeDtypeStruct((insts, blocks, dof, wide), jnp.bfloat16),
        in_specs=specs,
        out_specs=state,
        scratch_shapes=[pltpu.VMEM((rows, wide), jnp.float32)],
        input_output_aliases=aliases,
        cost_estimate=pl.CostEstimate(
            flops=20 * blocks * rows * wide,
            bytes_accessed=10 * blocks * rows * wide,
            transcendentals=0,
        ),
        compiler_params=pltpu.CompilerParams(vmem_limit_bytes=limit << 20),
    )(*operands)


def last_kernel(inst, row_low, left, right, base, step, far, arrived, old, out_hbm, total, out, sem):
    _, blocks, rows, wide = base.shape
    first = blocks - far.shape[1]
    odd = parity()
    slots = [(arrived, s, s) for s in range(arrived.shape[1])]
    faces = [face_of(left, right, s, odd) for _, _, s in slots]

    def write(block):
        target = out_hbm.at[inst, block, pl.ds(row_low, rows)]
        return pltpu.make_async_copy(out.at[block], target, sem.at[block])

    for block in range(blocks):
        chosen = [face == block for face in faces]
        spread = jnp.concatenate([step[block]] * (wide // 128), axis=-1)
        update(
            base.at[0, block], spread, far.at[0], slots, chosen, block, first,
            out.at[block], total,
        )
        write(block).start()
    for block in range(blocks):
        write(block).wait()


def last_part(inst, row_low, left, right, base, step, far, arrived, out):
    _, blocks, rows, wide = base.shape
    near_by = [pltpu.with_memory_space_constraint(x, pltpu.VMEM) for x in (far, arrived)]
    return pl.pallas_call(
        functools.partial(last_kernel, inst, row_low),
        out_shape=jax.ShapeDtypeStruct(out.shape, jnp.bfloat16),
        in_specs=[SMEM, SMEM, VMEM, VMEM, VMEM, VMEM, ANY],
        out_specs=ANY,
        scratch_shapes=[
            pltpu.VMEM((rows, wide), jnp.float32),
            pltpu.VMEM((blocks, rows, wide), jnp.bfloat16),
            pltpu.SemaphoreType.DMA((blocks,)),
        ],
        input_output_aliases={6: 0},
        cost_estimate=pl.CostEstimate(
            flops=20 * blocks * rows * wide,
            bytes_accessed=10 * blocks * rows * wide,
            transcendentals=0,
        ),
        compiler_params=pltpu.CompilerParams(vmem_limit_bytes=8 << 20),
        name="last",
    )(left, right, base, step, *near_by, out)


def per_device(adjoint, diag, off, off_columns, left, right, grad, step):
    insts, _, dof, _ = adjoint.shape
    iface = left.shape[1]
    parts, times = lax.axis_size("space"), lax.axis_size("tm")
    if times != 4 or insts != 2 or parts % 2:
        raise ValueError("unsupported mesh")
    instances = insts * times
    here = lax.axis_index("tm").astype(jnp.int32)[None]
    table = jnp.asarray(time_table(instances), dtype=jnp.float32)
    swap_core = [(i, i ^ 1) for i in range(times)]
    swap_chip = [(i, i ^ 2) for i in range(times)]
    pair = [(i, i ^ 1) for i in range(parts)]
    other = [(i, (i + 2 * (i % 2) - 1) % parts) for i in range(parts)]
    codes = off_columns.T
    cut, first, half = 256, 2, iface - 1

    ranges, pieces = [(0, half, iface - half)], [(0, iface - half, 0, dof)]
    pair0a, passed = remote_terms(0, iface, ranges, pieces, codes, adjoint, off, first)
    far0 = lax.ppermute(passed, "tm", swap_chip)
    from_pair0a = lax.ppermute(pair0a, "space", pair)
    near = lax.ppermute(adjoint, "tm", swap_core)
    ranges, pieces = [(0, 1, half - 1)], [(0, half - 1, 0, dof)]
    (pair0b,) = remote_terms(0, iface, ranges, pieces, codes, adjoint, off)
    from_pair0b = lax.ppermute(pair0b, "space", pair)
    ranges = [(1, 0, iface), (0, 0, 1)]
    pieces = [(0, iface, 0, dof), (iface, iface + 1, 0, dof)]
    other0, pair0c = remote_terms(0, iface, ranges, pieces, codes, adjoint, off)
    from_other0 = lax.ppermute(other0, "space", other)
    from_pair0c = lax.ppermute(pair0c, "space", pair)
    mixed = mix(here, table, adjoint, near, first, [(0, 0, dof), (1, 0, cut), (1, cut, dof)])
    far1 = lax.ppermute(mixed[0], "tm", swap_chip)
    far2a = lax.ppermute(mixed[1], "tm", swap_chip)
    far2b = lax.ppermute(mixed[2], "tm", swap_chip)
    ranges = [(1, 0, iface), (0, 0, iface)]
    pieces = [(0, iface, 0, dof), (iface, 2 * iface, 0, cut), (iface, 2 * iface, cut, dof)]
    other1, pair1a, pair1b = remote_terms(1, iface, ranges, pieces, codes, adjoint, off)
    from_other1 = lax.ppermute(other1, "space", other)
    from_pair1a = lax.ppermute(pair1a, "space", pair)
    from_pair1b = lax.ppermute(pair1b, "space", pair)
    relay = lax.ppermute(far0, "tm", swap_core)
    step = step[..., None]
    common = (codes, here, table, left, right, adjoint, near, far0, relay)
    (base0,) = local_part(0, 0, *common, from_other0, diag, off, grad, step)
    base1, base1b, step1b = local_part(1, dof - cut, *common, from_other1, diag, off, grad, step)
    faces = (left, right)
    arrivals = [(half, from_pair0a), (1, from_pair0b), (0, from_pair0c)]
    out = final_part(0, 0, dof, 2, *faces, base0, step, far1, arrivals, 58, None)
    out = final_part(1, 0, cut, 4, *faces, base1, step, far2a, [(0, from_pair1a)], 58, out)
    return last_part(1, cut, *faces, base1b, step1b, far2b, from_pair1b, out)


def solution(mesh):
    in_specs = (
        P("tm", "space", None, None),
        P("tm", "space", None, None),
        P("tm", "space", None, None, None),
        P("space", None),
        P("space", None),
        P("space", None),
        P("tm", "space", None, None),
        P("tm", "space", None),
    )
    out_specs = P("tm", "space", None, None)
    return jax.shard_map(
        per_device, mesh=mesh, in_specs=in_specs, out_specs=out_specs, check_vma=False
    )
```
